128 devices in a mesh: grp: 4 (over y), dp: 32 (over x, z, core).
Axes of the slice: x: 4, y: 4, z: 4, core: 2. Of those that a mesh axis runs over, the one named last changes fastest.
Arguments:
- hidden: bfloat16 [49152, 3584], P(('grp', 'dp')), may hold values from -250 to 250
- norm_gain: bfloat16 [3584], replicated, may hold values from 0.099609375 to 1.8984375
- w_qkv: bfloat16 [3584, 2304], P('dp'), may hold values from -0.09375 to 0.09375
- qkv_bias: bfloat16 [2304], replicated, may hold values from -3 to 3
- kv_cache: bfloat16 [32, 8192, 512], P(None, ('grp', 'dp')), may hold values from -200 to 200
- prompt_len: int32 [32], replicated, may hold values from 2048 to 8192, as said below
- serve_prompt: int32 [32], replicated, may hold values from 0 to 31, each once
- resp_live: int32 [3072], P(('grp', 'dp')), may hold values from 1 to 16, as said below
Outputs:
- attended: bfloat16 [49152, 1792], P(('grp', 'dp'))
The draws below stay inside these ranges and needn't reach their ends.
Inputs may be any that keep to these rules, and one draw needn't show every extreme that they name: `prompt_len`: at least one prompt has 8192 tokens. `serve_prompt`: each prompt is listed once. `resp_live`: some response has all 16 slots live.
All inputs are finite; a program needn't handle non-finite values.
Results may differ from the reference program's by a relative error of at most 0.012.
The reference program's roundings to bfloat16 on the way (of `normed`) count: a program that leaves them out, or rounds other values in their place, can miss the bound.
Values may be sent and summed in bfloat16 or wider, within the bound.
A program may use at most 128 MiB of HBM per device.

```python
import math
import jax
import jax.numpy as jnp
from jax import lax

D = 3584
HEADS = 14
KV_HEADS = 2
HEAD_DIM = 128
SPAN = 16
CAP = 8192
KB = 512
RESP_DEV = 24
TOK_DEV = 384
RESPONSES = 3072
TOKENS = 49152
PROMPTS = 32
PMIN = 2048
QKVW = 2304
N_DP = 32
DEVICES = 128


def draw_hidden(key, part):
    k_base, k_rows, k_cols = jax.random.split(key, 3)
    base = jnp.clip(jax.random.normal(k_base, (TOKENS, D), jnp.float32), -6.0, 6.0)
    row_scale = jnp.exp(jax.random.uniform(k_rows, (TOKENS, 1), jnp.float32, 0.0, math.log(10.0)))
    col_scale = jnp.exp(jax.random.uniform(k_cols, (1, D), jnp.float32, 0.0, math.log(4.0)))
    return (base * row_scale * col_scale).astype(jnp.bfloat16)


def draw_kv_cache(key, part):
    k_base = jax.random.fold_in(key, 0)
    width = KV_HEADS * HEAD_DIM
    column = jnp.arange(2 * width, dtype=jnp.int32)
    spread = jnp.where(column < width, 1.5, 3.0).astype(jnp.float32)
    base = jnp.clip(jax.random.normal(k_base, (PROMPTS, CAP, 2 * width), jnp.float32), -6.0, 6.0) * spread
    return base.astype(jnp.bfloat16)


def draw_prompt_len(key, part):
    k_len, k_on, k_pick = jax.random.split(key, 3)
    extra = jax.random.randint(k_len, (PROMPTS,), 0, CAP - PMIN + 1)
    longer = jax.random.randint(k_on, (PROMPTS,), 0, 4) == 0
    lengths = PMIN + jnp.where(longer, extra, 0)
    chosen = jax.random.randint(k_pick, (), 0, PROMPTS)
    return jnp.where(jnp.arange(PROMPTS, dtype=jnp.int32) == chosen, CAP, lengths).astype(jnp.int32)


def draw_resp_live(key, part):
    k_live, k_pick = jax.random.split(key)
    counts = jax.random.randint(k_live, (RESPONSES,), 1, SPAN + 1)
    chosen = jax.random.randint(k_pick, (), 0, RESPONSES)
    return jnp.where(jnp.arange(RESPONSES, dtype=jnp.int32) == chosen, SPAN, counts).astype(jnp.int32)


def shard_levels(rng, dims, shards, low, high):
    gain = 1.0
    for dim, blocks in shards:
        steps = jax.random.uniform(jax.random.fold_in(jax.random.fold_in(rng, 6), dim), (blocks,), jnp.float32, low / len(shards), high / len(shards))
        gain = gain * jnp.repeat(jnp.exp(steps), dims[dim] // blocks).reshape((-1,) + (1,) * (len(dims) - 1 - dim))
    return gain


def centred(rng, shape, scale, bound, cuts=(), held_as=jnp.bfloat16):
    drawn = jax.random.normal(rng, shape, jnp.float32) * scale
    if len(cuts) > 0:
        drawn = shard_levels(rng, shape, cuts, -0.22, 0.18) * drawn
    return jnp.clip(drawn, min=-bound, max=bound).astype(held_as)


def setup_inputs(seed: int = 0) -> dict:
    key_of = jax.random.split(jax.random.key(seed), 9)
    return {
        "hidden": draw_hidden(jax.random.fold_in(key_of[8], 71), 0),
        "norm_gain": jnp.clip(1.0 + 0.18 * jax.random.normal(key_of[1], (D,), jnp.float32), 0.099609375, 1.8984375).astype(jnp.bfloat16),
        "w_qkv": centred(key_of[2], (D, QKVW), D ** -0.5, 0.09375, ((0, 32),)),
        "qkv_bias": centred(key_of[3], (QKVW,), 0.5, 3.0),
        "kv_cache": draw_kv_cache(jax.random.fold_in(key_of[8], 71), 0),
        "prompt_len": draw_prompt_len(jax.random.fold_in(key_of[8], 71), 0),
        "serve_prompt": jax.random.permutation(key_of[6], PROMPTS).astype(jnp.int32),
        "resp_live": draw_resp_live(jax.random.fold_in(key_of[8], 71), 0),
    }


ROPE_BASE = 1000000.0
EPSILON = 1e-06

def normalize(hidden, norm_gain):
    values = hidden.astype(jnp.float32)
    spread = lax.rsqrt(lax.optimization_barrier(jnp.mean(values * values, axis=-1, keepdims=True)) + EPSILON)
    return (values * spread * norm_gain.astype(jnp.float32)).astype(jnp.bfloat16)

def rotate(values, position):
    half_dim = values.shape[-1] // 2
    steps_range = jnp.arange(half_dim, dtype=jnp.float32)
    inverse = jnp.exp(steps_range * (-2.0 * math.log(ROPE_BASE) / values.shape[-1]))
    angles = position[:, None] * inverse[None, :]
    cosine = jnp.cos(angles)[:, None, :]
    sine_part = jnp.sin(angles)[:, None, :]
    first_half = values[..., :half_dim]
    second_half = values[..., half_dim:]
    return jnp.concatenate([first_half * cosine - second_half * sine_part, second_half * cosine + first_half * sine_part], axis=-1)

def absorb(carry_state, scores, weigh):
    highest, running, weighted = carry_state
    new_top = jnp.maximum(highest, lax.optimization_barrier(jnp.max(scores, axis=-1)))
    weights = jnp.exp(scores - new_top[..., None]).astype(jnp.bfloat16)
    factor = jnp.exp(highest - new_top)
    running = running * factor + lax.optimization_barrier(jnp.sum(weights.astype(jnp.float32), axis=-1))
    weighted = weighted * factor[..., None] + weigh(weights)
    return (new_top, running, weighted)

def attend(projected, prompt_cache, length, live_count):
    count_rows = projected.shape[0]
    query_width = HEADS * HEAD_DIM
    kv_width = KV_HEADS * HEAD_DIM
    group_size = HEADS // KV_HEADS
    responses = count_rows // SPAN
    within = jnp.arange(count_rows, dtype=jnp.int32) % SPAN
    position = (length + within).astype(jnp.float32)
    query = rotate(projected[:, :query_width].reshape(count_rows, HEADS, HEAD_DIM), position).astype(jnp.bfloat16)
    key_new = rotate(projected[:, query_width:query_width + kv_width].reshape(count_rows, KV_HEADS, HEAD_DIM), position).astype(jnp.bfloat16)
    value_new = projected[:, query_width + kv_width:].reshape(count_rows, KV_HEADS, HEAD_DIM).astype(jnp.bfloat16)
    grouped = query.reshape(count_rows, KV_HEADS, group_size, HEAD_DIM).astype(jnp.float32)
    score_scale = 1.0 / math.sqrt(HEAD_DIM)
    carry_state = (jnp.full((KV_HEADS, group_size, count_rows), -jnp.inf, jnp.float32), jnp.zeros((KV_HEADS, group_size, count_rows), jnp.float32), jnp.zeros((KV_HEADS, group_size, count_rows, HEAD_DIM), jnp.float32))
    blocks = prompt_cache.reshape(CAP // KB, KB, 2 * kv_width)
    block_starts = jnp.arange(CAP // KB, dtype=jnp.int32) * KB

    def block_step(carry_state, block_item):
        key_block, block_start = block_item
        key_rows = key_block[:, :kv_width].reshape(KB, KV_HEADS, HEAD_DIM).astype(jnp.float32)
        value_rows = key_block[:, kv_width:].reshape(KB, KV_HEADS, HEAD_DIM).astype(jnp.float32)
        scores = jnp.einsum('tgsd,kgd->gstk', grouped, key_rows) * score_scale
        live_key = block_start + jnp.arange(KB, dtype=jnp.int32) < length
        scores = jnp.where(live_key, scores, -jnp.inf)

        def weigh(weights):
            return jnp.einsum('gstk,kgd->gstd', weights.astype(jnp.float32), value_rows)
        return (absorb(carry_state, scores, weigh), None)
    carry_state, _ = lax.scan(block_step, carry_state, (blocks, block_starts))
    query_own = grouped.reshape(responses, SPAN, KV_HEADS, group_size, HEAD_DIM)
    key_own = key_new.reshape(responses, SPAN, KV_HEADS, HEAD_DIM).astype(jnp.float32)
    value_own = value_new.reshape(responses, SPAN, KV_HEADS, HEAD_DIM).astype(jnp.float32)
    own_scores = jnp.einsum('rigsd,rjgd->gsrij', query_own, key_own) * score_scale
    causal = jnp.arange(SPAN)[None, :] <= jnp.arange(SPAN)[:, None]
    own_scores = jnp.where(causal, own_scores, -jnp.inf).reshape(KV_HEADS, group_size, count_rows, SPAN)

    def weigh_own(weights):
        shaped = weights.astype(jnp.float32).reshape(KV_HEADS, group_size, responses, SPAN, SPAN)
        return jnp.einsum('gsrij,rjgd->gsrid', shaped, value_own).reshape(KV_HEADS, group_size, count_rows, HEAD_DIM)
    highest, running, weighted = absorb(carry_state, own_scores, weigh_own)
    result = weighted / running[..., None]
    result = jnp.transpose(result, (2, 0, 1, 3)).reshape(count_rows, HEADS * HEAD_DIM)
    response_id = jnp.arange(count_rows, dtype=jnp.int32) // SPAN
    keep_row = within < live_count[response_id]
    return jnp.where(keep_row[:, None], result, 0.0).astype(jnp.bfloat16)

def reference(hidden, norm_gain, w_qkv, qkv_bias, kv_cache, prompt_len, serve_prompt, resp_live):
    normed = normalize(hidden, norm_gain)
    projected = jnp.dot(normed, w_qkv, preferred_element_type=jnp.float32) + qkv_bias.astype(jnp.float32)
    device_rows = projected.reshape(DEVICES, TOK_DEV, QKVW)
    device_live = resp_live.reshape(DEVICES, RESP_DEV)

    def per_device(device_item):
        rows_here, live_here, device_id = device_item
        prompt = serve_prompt[device_id % N_DP]
        return attend(rows_here, kv_cache[prompt], prompt_len[prompt], live_here)
    attended = lax.map(per_device, (device_rows, device_live, jnp.arange(DEVICES, dtype=jnp.int32)))
    return attended.reshape(TOKENS, HEADS * HEAD_DIM)
```

```python
import math

import jax
import jax.numpy as jnp
from jax import lax
from jax.experimental import pallas as pl
from jax.experimental.pallas import tpu as pltpu
from jax.sharding import PartitionSpec as P

D = 3584
HEADS = 14
GROUP = 7
HEAD_DIM = 128
SPAN = 16
CAP = 8192
TOK = 384
STRIPE = 112
GW = 1152
PLANE = 2048
SLICE = 64
TILE = 128
TQ = GROUP * TILE
TILES = TOK // TILE
KB = 512
STEP = 2 * KB
FIRST = 64
ROPE_BASE = 1000000.0
EPSILON = 1e-06
FOLD = math.log2(math.e) / math.sqrt(HEAD_DIM)
MESH = pl.DeviceIdType.MESH
OFFSETS = (0, 1, 3, 2)
VMEM_LIMIT = 64 * 1000 * 1000


def exchange(
    w_src,
    kv_src,
    hid,
    w_out,
    kv_out,
    hid_out,
    local_sem,
    pair_send,
    pair_recv,
    kv_send,
    kv_recv,
    y_send,
    y_recv,
    w_send,
    w_recv,
):
    y = lax.axis_index("grp")
    d = lax.axis_index("dp")
    core = lax.rem(d, 2)
    z = lax.rem(d // 2, 4)
    x = d // 8
    up = lax.rem(y + 1, 4)
    down = lax.rem(y + 3, 4)
    partner = d + 1 - 2 * core

    barrier = pltpu.get_barrier_semaphore()

    def greet(k, carry):
        pl.semaphore_signal(
            barrier, inc=1, device_id=(y, lax.rem(d + k, 32)), device_id_type=MESH
        )
        return carry

    lax.fori_loop(1, 32, greet, 0)
    for other in (up, down):
        pl.semaphore_signal(barrier, inc=1, device_id=(other, d), device_id_type=MESH)
    pl.semaphore_wait(barrier, 33)

    def stripe(row, rows):
        return w_out.at[pl.ds(pl.multiple_of(row, 16), rows), :]

    def remote(src, dst, send, recv, target):
        return pltpu.make_async_remote_copy(
            src_ref=src,
            dst_ref=dst,
            send_sem=send,
            recv_sem=recv,
            device_id=target,
            device_id_type=MESH,
        )

    def kv_rows(plane, source):
        return pl.ds(pl.multiple_of(plane * PLANE + source * SLICE, SLICE), SLICE)

    my_row = d * STRIPE
    keep_w = pltpu.make_async_copy(w_src.at[core], stripe(my_row, STRIPE), local_sem.at[0])
    keep_w.start()
    keep_kv = pltpu.make_async_copy(
        kv_src.at[d // 2, core], kv_out.at[:, kv_rows(y, d), :], local_sem.at[1]
    )
    keep_kv.start()
    give_w = remote(
        w_src.at[1 - core], stripe(my_row, STRIPE), pair_send.at[0], pair_recv.at[0], (y, partner)
    )
    give_w.start()
    take_w = remote(
        w_src.at[1 - core],
        stripe(partner * STRIPE, STRIPE),
        pair_send.at[0],
        pair_recv.at[0],
        (y, partner),
    )
    give_h = remote(hid, hid_out, pair_send.at[1], pair_recv.at[1], (y, partner))
    give_h.start()

    def kv_copy(k, source, target):
        return remote(
            kv_src.at[target // 2, lax.rem(target, 2)],
            kv_out.at[:, kv_rows(y, source), :],
            kv_send.at[k],
            kv_recv.at[k],
            (y, target),
        )

    def kv_start(k, carry):
        kv_copy(k, d, lax.rem(d + k, 32)).start()
        return carry

    lax.fori_loop(1, 32, kv_start, 0)

    def place(h, first, second):
        if h == 0:
            return (lax.rem(first, 4) * 8 + lax.rem(second, 4) * 2) * STRIPE
        return (lax.rem(second, 4) * 8 + lax.rem(first, 4) * 2 + 1) * STRIPE

    def along(h, phase, shift):
        if (h == 0) == (phase == 1):
            return (y, lax.rem(x + shift, 4) * 8 + z * 2 + core)
        return (y, x * 8 + lax.rem(z + shift, 4) * 2 + core)

    def mine(h):
        return (x, z) if h == 0 else (z, x)

    def w_block(h, stage, kind, row):
        if kind == 2:
            return stripe(row, FIRST)
        if kind == 3:
            return stripe(row + FIRST, STRIPE - FIRST)
        return stripe(row, STRIPE)

    def w_out_copy(h, stage, kind, row):
        phase = 1 if stage == 0 else 2
        shift = 1 if kind in (0, 2) else 3
        ref = w_block(h, stage, kind, row)
        return remote(
            ref, ref, w_send.at[h, stage, kind], w_recv.at[h, stage, kind], along(h, phase, shift)
        )

    def w_row(h, stage, kind):
        first, second = mine(h)
        back = {0: 3, 1: 1, 2: 2, 3: 2}[kind]
        if stage == 0:
            return place(h, first + back, second)
        return place(h, first + OFFSETS[stage - 1], second + back)

    def w_wait(stage, kinds):
        for h in (0, 1):
            for kind in kinds:
                w_out_copy(h, stage, kind, w_row(h, stage, kind)).wait_recv()

    def w_start(stage):
        for h in (0, 1):
            first, second = mine(h)
            row = place(h, first, second)
            if stage > 0:
                row = place(h, first + OFFSETS[stage - 1], second)
            for kind in (0, 1):
                w_out_copy(h, stage, kind, row).start()

    def w_forward(stage):
        for h in (0, 1):
            for kind in (0, 1):
                w_out_copy(h, stage, kind + 2, w_row(h, stage, kind)).start()

    keep_w.wait()
    take_w.wait_recv()
    w_start(0)
    w_start(1)
    keep_kv.wait()

    def y_copy(kind, k, plane, source):
        rows = kv_rows(plane, source)
        if kind == 2:
            ref = kv_out.at[0, rows, :]
        elif kind == 3:
            ref = kv_out.at[1, rows, :]
        else:
            ref = kv_out.at[:, rows, :]
        target = (up, d) if kind in (0, 2) else (down, d)
        return remote(ref, ref, y_send.at[kind, k], y_recv.at[kind, k], target)

    def spread(k):
        source = lax.rem(d + 32 - k, 32)
        y_copy(0, k, y, source).start()
        y_copy(1, k, y, source).start()

    def relay(k):
        source = lax.rem(d + 32 - k, 32)
        y_copy(0, k, down, source).wait_recv()
        y_copy(2, k, down, source).start()
        y_copy(1, k, up, source).wait_recv()
        y_copy(3, k, up, source).start()

    def spread_step(k, carry):
        kv_copy(k, lax.rem(d + 32 - k, 32), d).wait_recv()
        spread(k)
        return carry

    def relay_step(k, carry):
        relay(k)
        return carry

    spread(0)
    lax.fori_loop(1, 8, spread_step, 0)
    w_wait(0, (0, 1))
    w_forward(0)
    w_start(2)
    w_start(3)
    lax.fori_loop(8, 16, spread_step, 0)
    w_wait(1, (0, 1))
    w_forward(1)
    lax.fori_loop(16, 24, spread_step, 0)
    w_wait(0, (2, 3))
    w_start(4)
    lax.fori_loop(24, 32, spread_step, 0)
    lax.fori_loop(0, 8, relay_step, 0)
    w_wait(2, (0, 1))
    w_forward(2)
    lax.fori_loop(8, 16, relay_step, 0)
    w_wait(3, (0, 1))
    w_forward(3)
    lax.fori_loop(16, 24, relay_step, 0)
    w_wait(4, (0, 1))
    w_forward(4)
    lax.fori_loop(24, 32, relay_step, 0)
    for stage in (1, 2, 3, 4):
        w_wait(stage, (2, 3))

    def finish(k, carry):
        source = lax.rem(d + 32 - k, 32)
        opposite = lax.rem(y + 2, 4)
        y_copy(2, k, opposite, source).wait_recv()
        y_copy(3, k, opposite, source).wait_recv()
        y_copy(0, k, y, source).wait_send()
        y_copy(1, k, y, source).wait_send()
        y_copy(2, k, down, source).wait_send()
        y_copy(3, k, up, source).wait_send()
        return carry

    lax.fori_loop(0, 32, finish, 0)

    def drain(k, carry):
        kv_copy(k, d, lax.rem(d + k, 32)).wait_send()
        return carry

    lax.fori_loop(1, 32, drain, 0)
    for stage in range(5):
        for h in (0, 1):
            for kind in range(4):
                w_out_copy(h, stage, kind, w_row(h, stage, kind)).wait_send()
    give_w.wait_send()
    give_h.wait()


def communicate(w_src, kv_src, hidden):
    any_spec = pl.BlockSpec(memory_space=pl.ANY)
    vmem_spec = pl.BlockSpec(memory_space=pltpu.VMEM)
    dma = pltpu.SemaphoreType.DMA
    return pl.pallas_call(
        exchange,
        out_shape=(
            jax.ShapeDtypeStruct((D, GW), jnp.bfloat16),
            jax.ShapeDtypeStruct((2, CAP, 2 * HEAD_DIM), jnp.bfloat16),
            jax.ShapeDtypeStruct((TOK, D), jnp.bfloat16),
        ),
        in_specs=[vmem_spec, vmem_spec, any_spec],
        out_specs=(any_spec, any_spec, any_spec),
        scratch_shapes=[
            dma((2,)),
            dma((2,)),
            dma((2,)),
            dma((32,)),
            dma((32,)),
            dma((4, 32)),
            dma((4, 32)),
            dma((2, 5, 4)),
            dma((2, 5, 4)),
        ],
        compiler_params=pltpu.CompilerParams(collective_id=0, has_side_effects=True),
        name="exchange",
    )(w_src, kv_src, hidden)


def project_kernel(hid_a, hid_b, gain, w, bias, cos, sin, q_out, kv_out, normed):
    for s, hid in enumerate((hid_a, hid_b)):

        def norm_rows(i, carry):
            rows = pl.ds(pl.multiple_of(i * 32, 32), 32)
            values = hid[rows, :].astype(jnp.float32)
            spread = lax.rsqrt(jnp.mean(values * values, axis=-1, keepdims=True) + EPSILON)
            normed[rows, :] = (values * spread * gain[...]).astype(jnp.bfloat16)
            return carry

        lax.fori_loop(0, TOK // 32, norm_rows, 0)

        def columns(n, carry):
            cols = pl.ds(pl.multiple_of(n * 384, 384), 384)
            part = jnp.dot(normed[...], w[:, cols], preferred_element_type=jnp.float32)
            part = part + bias[:, cols]
            for u in range(3):
                head = part[:, u * HEAD_DIM : (u + 1) * HEAD_DIM]
                turned = head * cos[s] + pltpu.roll(head, HEAD_DIM // 2, 1) * sin[s]
                index = n * 3 + u
                if u == 2:
                    head = jnp.where(n == 2, head, turned)
                else:
                    head = turned
                head = head.astype(jnp.bfloat16)
                if u == 0:
                    for t in range(TILES):
                        q_out[s, t, pl.ds(pl.multiple_of(index * TILE, TILE), TILE), :] = head[
                            t * TILE : (t + 1) * TILE
                        ]
                else:

                    @pl.when(n < 2)
                    def _():
                        for t in range(TILES):
                            q_out[s, t, pl.ds(pl.multiple_of(index * TILE, TILE), TILE), :] = head[
                                t * TILE : (t + 1) * TILE
                            ]

                    @pl.when(n == 2)
                    def _():
                        kv_out[s, :, (u - 1) * HEAD_DIM : u * HEAD_DIM] = head

            return carry

        lax.fori_loop(0, 3, columns, 0)


def project(hid_a, hid_b, gain, w, bias, cos, sin):
    vmem_spec = pl.BlockSpec(memory_space=pltpu.VMEM)
    return pl.pallas_call(
        project_kernel,
        out_shape=(
            jax.ShapeDtypeStruct((2, TILES, TQ, HEAD_DIM), jnp.bfloat16),
            jax.ShapeDtypeStruct((2, TOK, 2 * HEAD_DIM), jnp.bfloat16),
        ),
        in_specs=[vmem_spec] * 7,
        out_specs=(vmem_spec, vmem_spec),
        scratch_shapes=[pltpu.VMEM((TOK, D), jnp.bfloat16)],
        compiler_params=pltpu.CompilerParams(vmem_limit_bytes=VMEM_LIMIT),
        name="project",
    )(hid_a, hid_b, gain, w, bias, cos, sin)


def attend_kernel(info, q, own, kv, out, kv_buf, scores, sems):
    which = info[0]
    length = info[1]
    blocks = (length + STEP - 1) // STEP
    full = length // STEP

    def load(j):
        rows = pl.ds(pl.multiple_of(j * STEP, STEP), STEP)
        return pltpu.make_async_copy(kv.at[which, rows, :], kv_buf.at[rows, :], sems.at[j])

    def load_start(j, carry):
        load(j).start()
        return carry

    lax.fori_loop(0, blocks, load_start, 0)
    ones = jnp.ones((KB, 8), jnp.bfloat16)

    def tile(t, carry):
        query = q[t]

        def score(j, slot):
            keys = kv_buf[pl.ds(pl.multiple_of(j * KB, KB), KB), :HEAD_DIM]
            scores[slot] = lax.dot_general(
                keys, query, (((1,), (1,)), ((), ())), preferred_element_type=jnp.float32
            )

        def absorb(state, raw, values, ones):
            top, acc = state
            new_top = jnp.maximum(top, jnp.max(raw, axis=0, keepdims=True))
            weights = jnp.exp2((raw - new_top) * FOLD).astype(jnp.bfloat16)
            factor = jnp.exp2((top - new_top) * FOLD)
            wide = jnp.concatenate([values, ones], axis=1)
            acc = acc * factor + lax.dot_general(
                wide, weights, (((0,), (0,)), ((), ())), preferred_element_type=jnp.float32
            )
            return new_top, acc

        def half(j, slot, state, masked):
            score(jnp.minimum(j + 1, 2 * blocks - 1), 1 - slot)
            raw = scores[slot]
            if masked:
                row = j * KB + lax.broadcasted_iota(jnp.int32, (KB, 1), 0)
                raw = jnp.where(row < length, raw, -jnp.inf)
            values = kv_buf[pl.ds(pl.multiple_of(j * KB, KB), KB), HEAD_DIM:]
            return absorb(state, raw, values, ones)

        def step(i, state, masked):
            @pl.when((t == 0) & (i + 1 < blocks))
            def _():
                load(i + 1).wait()

            state = half(2 * i, 0, state, masked)
            return half(2 * i + 1, 1, state, masked)

        own_rows = pl.ds(pl.multiple_of(t * TILE, TILE), TILE)
        raw = lax.dot_general(
            own[own_rows, :HEAD_DIM],
            query,
            (((1,), (1,)), ((), ())),
            preferred_element_type=jnp.float32,
        )
        key_id = lax.broadcasted_iota(jnp.int32, (TILE, TQ), 0)
        query_id = lax.rem(lax.broadcasted_iota(jnp.int32, (TILE, TQ), 1), TILE)
        seen = (key_id // SPAN == query_id // SPAN) & (key_id <= query_id)
        raw = jnp.where(seen, raw, -jnp.inf)
        state = (
            jnp.full((1, TQ), -jnp.inf, jnp.float32),
            jnp.zeros((HEAD_DIM + 8, TQ), jnp.float32),
        )
        state = absorb(state, raw, own[own_rows, HEAD_DIM:], ones[:TILE])

        @pl.when(t == 0)
        def _():
            load(0).wait()

        score(0, 0)
        state = lax.fori_loop(0, full, lambda i, state: step(i, state, False), state)
        state = lax.fori_loop(full, blocks, lambda i, state: step(i, state, True), state)
        _, acc = state
        result = acc[:HEAD_DIM] / acc[HEAD_DIM : HEAD_DIM + 1]
        for h in range(GROUP):
            out[own_rows, h * HEAD_DIM : (h + 1) * HEAD_DIM] = result[
                :, h * TILE : (h + 1) * TILE
            ].T.astype(jnp.bfloat16)
        return carry

    lax.fori_loop(0, TILES, tile, 0)


def attend(info, q, own, kv):
    vmem_spec = pl.BlockSpec(memory_space=pltpu.VMEM)
    return pl.pallas_call(
        attend_kernel,
        out_shape=jax.ShapeDtypeStruct((TOK, GROUP * HEAD_DIM), jnp.bfloat16),
        in_specs=[
            pl.BlockSpec(memory_space=pltpu.SMEM),
            vmem_spec,
            vmem_spec,
            pl.BlockSpec(memory_space=pl.ANY),
        ],
        out_specs=vmem_spec,
        scratch_shapes=[
            pltpu.VMEM((CAP, 2 * HEAD_DIM), jnp.bfloat16),
            pltpu.VMEM((2, KB, TQ), jnp.float32),
            pltpu.SemaphoreType.DMA((CAP // STEP,)),
        ],
        compiler_params=pltpu.CompilerParams(vmem_limit_bytes=40 * 1000 * 1000),
        cost_estimate=pl.CostEstimate(
            flops=4 * TOK * GROUP * HEAD_DIM * CAP,
            bytes_accessed=4 * CAP * HEAD_DIM,
            transcendentals=TOK * GROUP * CAP,
        ),
        name="attend",
    )(info, q, own, kv)


def by_group(array):
    width = GROUP * HEAD_DIM
    kv = 2 * HEADS * HEAD_DIM // 2
    parts = []
    for c in range(2):
        base = HEADS * HEAD_DIM + c * HEAD_DIM
        parts.append(
            jnp.concatenate(
                [
                    array[..., c * width : (c + 1) * width],
                    array[..., base : base + HEAD_DIM],
                    array[..., base + 2 * HEAD_DIM : base + 3 * HEAD_DIM],
                ],
                axis=-1,
            )
        )
    return jnp.stack(parts)


def angles(length):
    steps_range = jnp.arange(HEAD_DIM // 2, dtype=jnp.float32)
    inverse = jnp.exp(steps_range * (-2.0 * math.log(ROPE_BASE) / HEAD_DIM))
    position = (length[:, None] + jnp.arange(SPAN, dtype=jnp.int32)[None, :]).astype(jnp.float32)
    turn = position[:, :, None] * inverse
    cos = jnp.cos(turn)
    sin = jnp.sin(turn)
    cos = jnp.concatenate([cos, cos], axis=-1)
    sin = jnp.concatenate([-sin, sin], axis=-1)
    reps = (1, TOK // SPAN, 1)
    return jnp.tile(cos, reps), jnp.tile(sin, reps)


def shards(hidden, norm_gain, w_qkv, qkv_bias, kv_cache, prompt_len, serve_prompt, resp_live):
    d = lax.axis_index("dp")
    core = d % 2
    w_src = by_group(w_qkv)
    bias = by_group(qkv_bias.astype(jnp.float32)[None, :])[core]
    picked = jnp.take(kv_cache, serve_prompt, axis=0)
    picked = picked.reshape(16, 2, SLICE, 2, 2, HEAD_DIM)
    kv_src = jnp.transpose(picked, (0, 4, 1, 2, 3, 5)).reshape(16, 2, 2, SLICE, 2 * HEAD_DIM)
    w_full, kv_full, other = communicate(w_src, kv_src, hidden)
    sides = jnp.stack([core, 1 - core])
    lengths = prompt_len[serve_prompt[d - core + sides]]
    cos, sin = angles(lengths)
    q, own = project(
        hidden, other, norm_gain.astype(jnp.float32)[None, :], w_full, bias, cos, sin
    )
    far = attend(jnp.stack([sides[1], lengths[1]]), q[1], own[1], kv_full)
    arrived = lax.ppermute(far, "dp", [(i, i ^ 1) for i in range(32)])
    near = attend(jnp.stack([sides[0], lengths[0]]), q[0], own[0], kv_full)
    low = jnp.where(core == 0, near, arrived)
    high = jnp.where(core == 0, arrived, near)
    result = jnp.concatenate([low, high], axis=1)
    keep = (jnp.arange(SPAN, dtype=jnp.int32)[None, :] < resp_live[:, None]).reshape(TOK, 1)
    return jnp.where(keep, result, jnp.zeros((), jnp.bfloat16))


def solution(mesh):
    in_specs = (
        P(("grp", "dp"), None),
        P(),
        P("dp", None),
        P(),
        P(None, ("grp", "dp"), None),
        P(),
        P(),
        P(("grp", "dp")),
    )
    out_specs = P(("grp", "dp"), None)
    return jax.shard_map(shards, mesh=mesh, in_specs=in_specs, out_specs=out_specs, check_vma=False)
```

```python
import functools
import math

import jax
import jax.numpy as jnp
from jax import lax
from jax.experimental import pallas as pl
from jax.experimental.pallas import tpu as pltpu
from jax.sharding import PartitionSpec as P

D = 3584
HEADS = 14
GROUP = 7
HEAD_DIM = 128
SPAN = 16
CAP = 8192
TOK = 384
STRIPE = 112
GW = 1152
PLANE = 2048
SLICE = 64
TILE = 128
TQ = GROUP * TILE
TILES = TOK // TILE
KB = 512
STEP = 2 * KB
FIRST = 64
ROPE_BASE = 1000000.0
EPSILON = 1e-06
FOLD = math.log2(math.e) / math.sqrt(HEAD_DIM)
MESH = pl.DeviceIdType.MESH
OFFSETS = (0, 1, 3, 2)
VMEM_LIMIT = 64 * 1000 * 1000


def exchange(
    lens,
    serve,
    kv,
    w,
    hid,
    gain,
    bias,
    q_out,
    own_out,
    kv_out,
    w_buf,
    w_pack,
    kv_pack,
    hid_far,
    normed,
    bounce,
    local_sem,
    pair_send,
    pair_recv,
    kv_send,
    kv_recv,
    bounce_send,
    bounce_recv,
    y_send,
    y_recv,
    w_send,
    w_recv,
):
    y = lax.axis_index("grp")
    d = lax.axis_index("dp")
    core = lax.rem(d, 2)
    z = lax.rem(d // 2, 4)
    x = d // 8
    chip = d // 2
    up = lax.rem(y + 1, 4)
    down = lax.rem(y + 3, 4)
    opposite = lax.rem(y + 2, 4)
    partner = d + 1 - 2 * core

    barrier = pltpu.get_barrier_semaphore()

    def greet(k, carry):
        pl.semaphore_signal(
            barrier, inc=1, device_id=(y, lax.rem(d + k, 32)), device_id_type=MESH
        )
        return carry

    lax.fori_loop(1, 32, greet, 0)
    for other in (up, down):
        pl.semaphore_signal(barrier, inc=1, device_id=(other, d), device_id_type=MESH)

    width = GROUP * HEAD_DIM
    for c in range(2):
        base = HEADS * HEAD_DIM + c * HEAD_DIM
        w_pack[c, :, :width] = w[:, c * width : (c + 1) * width]
        w_pack[c, :, width : width + HEAD_DIM] = w[:, base : base + HEAD_DIM]
        w_pack[c, :, width + HEAD_DIM :] = w[:, base + 2 * HEAD_DIM : base + 3 * HEAD_DIM]

    def pack(j, carry):
        for p in range(2):
            rows = kv[serve[2 * j + p]]
            for c in range(2):
                for part in range(2):
                    col = (2 * part + c) * HEAD_DIM
                    kv_pack[j, c, p, :, part * HEAD_DIM : (part + 1) * HEAD_DIM] = rows[
                        :, col : col + HEAD_DIM
                    ]
        return carry

    lax.fori_loop(0, 16, pack, 0)
    pl.semaphore_wait(barrier, 33)

    def stripe(row, rows):
        return w_buf.at[pl.ds(pl.multiple_of(row, 16), rows), :]

    def remote(src, dst, send, recv, target):
        return pltpu.make_async_remote_copy(
            src_ref=src,
            dst_ref=dst,
            send_sem=send,
            recv_sem=recv,
            device_id=target,
            device_id_type=MESH,
        )

    def at(px, pz, pc):
        return lax.rem(px, 4) * 8 + lax.rem(pz, 4) * 2 + pc

    def kv_rows(plane, source):
        return pl.ds(pl.multiple_of(plane * PLANE + source * SLICE, SLICE), SLICE)

    my_row = d * STRIPE
    give_w = remote(
        w_pack.at[1 - core], stripe(my_row, STRIPE), pair_send.at[0], pair_recv.at[0], (y, partner)
    )
    give_w.start()
    take_w = remote(
        w_pack.at[1 - core],
        stripe(partner * STRIPE, STRIPE),
        pair_send.at[0],
        pair_recv.at[0],
        (y, partner),
    )
    keep_w = pltpu.make_async_copy(w_pack.at[core], stripe(my_row, STRIPE), local_sem.at[0])
    keep_w.start()
    keep_kv = pltpu.make_async_copy(
        kv_pack.at[chip, core], kv_out.at[:, kv_rows(y, d), :], local_sem.at[1]
    )
    keep_kv.start()

    def order(dx, dz):
        back = (0, 1, 3, 2)
        return 4 * back[dz] + back[dx]

    def kv_copy(k, cs, source, target):
        return remote(
            kv_pack.at[target // 2, lax.rem(target, 2)],
            kv_out.at[:, kv_rows(y, source), :],
            kv_send.at[k, lax.rem(target, 2)],
            kv_recv.at[k, cs],
            (y, target),
        )

    def bounce_in(slot, k, far, middle):
        return remote(
            kv_pack.at[far // 2, lax.rem(far, 2)],
            bounce.at[slot],
            kv_send.at[k, lax.rem(far, 2)],
            bounce_recv.at[slot],
            (y, middle),
        )

    def bounce_out(slot, k, cs, source, target):
        return remote(
            bounce.at[slot],
            kv_out.at[:, kv_rows(y, source), :],
            bounce_send.at[slot],
            kv_recv.at[k, cs],
            (y, target),
        )

    def outgoing(dx, dz, c2):
        k = order(dx, dz)
        far = at(x + dx, z + dz, c2)
        if dx == 2 and dz % 2 == 1:
            return bounce_in(dz // 2 * 2 + core, k, far, at(x + 3, z + dz, c2))
        if dz == 2 and dx % 2 == 1:
            return bounce_in(4 + dx // 2 * 2 + core, k, far, at(x + dx, z + 3, c2))
        return kv_copy(k, core, d, far)

    def bouncing():
        for i, step in enumerate((1, 3)):
            for cs in range(2):
                slot = 2 * i + cs
                source = at(x + 1, z + 4 - step, cs)
                yield slot, bounce_out(slot, order(2, step), cs, source, at(x + 3, z, core))
                slot = 4 + 2 * i + cs
                source = at(x + 4 - step, z + 1, cs)
                yield slot, bounce_out(slot, order(step, 2), cs, source, at(x, z + 3, core))

    sends = [(dx, dz) for dz in OFFSETS for dx in OFFSETS]
    give_kv = kv_copy(0, core, d, partner)
    ties = [t for t in sends if t in ((2, 1), (2, 3), (1, 2), (3, 2))]
    near = [t for t in sends if t in ((1, 0), (3, 0), (0, 1), (0, 3))]
    rest = [t for t in sends[1:] if t not in near and t not in ties]

    def issue(group):
        for dx, dz in group:
            for c2 in range(2):
                outgoing(dx, dz, c2).start()

    def place(h, first, second):
        if h == 0:
            return (lax.rem(first, 4) * 8 + lax.rem(second, 4) * 2) * STRIPE
        return (lax.rem(second, 4) * 8 + lax.rem(first, 4) * 2 + 1) * STRIPE

    def along(h, phase, shift):
        if (h == 0) == (phase == 1):
            return (y, at(x + shift, z, core))
        return (y, at(x, z + shift, core))

    def mine(h):
        return (x, z) if h == 0 else (z, x)

    def w_block(kind, row):
        if kind == 2:
            return stripe(row, FIRST)
        if kind == 3:
            return stripe(row + FIRST, STRIPE - FIRST)
        return stripe(row, STRIPE)

    def w_copy(h, stage, kind, row):
        phase = 1 if stage == 0 else 2
        shift = 1 if kind in (0, 2) else 3
        ref = w_block(kind, row)
        return remote(
            ref, ref, w_send.at[h, stage, kind], w_recv.at[h, stage, kind], along(h, phase, shift)
        )

    def w_row(h, stage, kind):
        first, second = mine(h)
        back = (3, 1, 2, 2)[kind]
        if stage == 0:
            return place(h, first + back, second)
        return place(h, first + OFFSETS[stage - 1], second + back)

    def w_wait(stage, kinds):
        for h in (0, 1):
            for kind in kinds:
                w_copy(h, stage, kind, w_row(h, stage, kind)).wait_recv()

    def w_start(stage):
        for h in (0, 1):
            first, second = mine(h)
            row = place(h, first, second)
            if stage > 0:
                row = place(h, first + OFFSETS[stage - 1], second)
            for kind in (0, 1):
                w_copy(h, stage, kind, row).start()

    def w_forward(stage):
        for h in (0, 1):
            for kind in (0, 1):
                w_copy(h, stage, kind + 2, w_row(h, stage, kind)).start()

    give_h = remote(hid, hid_far, pair_send.at[1], pair_recv.at[1], (y, partner))

    def gray(i):
        return i + i // 2 * (1 - 2 * lax.rem(i, 2))

    def chip_of(k):
        dx = gray(lax.rem(k, 4))
        dz = gray(k // 4)
        return lax.rem(x + 4 - dx, 4) * 4 + lax.rem(z + 4 - dz, 4)

    def chip_rows(plane, k):
        return pl.ds(pl.multiple_of(plane * PLANE + chip_of(k) * 2 * SLICE, SLICE), 2 * SLICE)

    def y_copy(kind, k, plane):
        rows = chip_rows(plane, k)
        if kind >= 2:
            ref = kv_out.at[kind - 2, rows, :]
        else:
            ref = kv_out.at[:, rows, :]
        target = (up, d) if kind in (0, 2) else (down, d)
        return remote(ref, ref, y_send.at[kind, k], y_recv.at[kind, k], target)

    def spread(k, carry):
        for cs in range(2):
            kv_copy(k, cs, chip_of(k) * 2 + cs, d).wait_recv()
        y_copy(0, k, y).start()
        y_copy(1, k, y).start()
        return carry

    def relay(k, carry):
        y_copy(0, k, down).wait_recv()
        y_copy(2, k, down).start()
        y_copy(1, k, up).wait_recv()
        y_copy(3, k, up).start()
        return carry

    def both(lag, k, carry):
        spread(k, carry)
        relay(k - lag, carry)
        return carry

    def norm(source, slot):
        def rows(i, carry):
            part = pl.ds(pl.multiple_of(i * 32, 32), 32)
            values = source[part, :].astype(jnp.float32)
            spread = lax.rsqrt(jnp.mean(values * values, axis=-1, keepdims=True) + EPSILON)
            scaled = values * spread * gain[...].astype(jnp.float32)
            normed[slot, part, :] = scaled.astype(jnp.bfloat16)
            return carry

        lax.fori_loop(0, TOK // 32, rows, 0)

    def first_spread():
        keep_kv.wait()
        kv_copy(0, 1 - core, partner, d).wait_recv()
        y_copy(0, 0, y).start()
        y_copy(1, 0, y).start()

    def begin_w():
        keep_w.wait()
        take_w.wait_recv()
        w_start(0)

    def hop(stage):
        w_wait(stage, (0, 1))
        w_forward(stage)

    def bounce_all():
        for slot, copy in bouncing():
            bounce_in(slot, 0, d, d).wait_recv()
            copy.start()

    def norm_far():
        give_h.wait_recv()
        norm(hid_far, 1 - core)

    give_kv.start()
    issue(near)
    issue(ties)
    issue(rest)
    begin_w()
    give_h.start()
    first_spread()
    lax.fori_loop(1, 4, spread, 0)
    bounce_all()
    lax.fori_loop(4, 16, spread, 0)
    hop(0)
    w_start(1)
    w_start(2)
    w_start(3)
    norm(hid, core)
    lax.fori_loop(0, 6, relay, 0)
    hop(1)
    norm_far()
    lax.fori_loop(6, 12, relay, 0)
    w_wait(0, (2, 3))
    w_start(4)
    hop(2)
    lax.fori_loop(12, 16, relay, 0)
    hop(3)
    hop(4)
    for stage in (1, 2, 3, 4):
        w_wait(stage, (2, 3))

    steps_range = lax.broadcasted_iota(jnp.int32, (SPAN, HEAD_DIM), 1)
    steps_range = jnp.where(
        steps_range < HEAD_DIM // 2, steps_range, steps_range - HEAD_DIM // 2
    ).astype(jnp.float32)
    inverse = jnp.exp(steps_range * (-2.0 * math.log(ROPE_BASE) / HEAD_DIM))
    flip = lax.broadcasted_iota(jnp.int32, (SPAN, HEAD_DIM), 1) < HEAD_DIM // 2
    slots = lax.broadcasted_iota(jnp.int32, (SPAN, HEAD_DIM), 0)

    def bias_at(low):
        both_sides = []
        for c in range(2):
            start = c * width + low
            if low >= width:
                start = HEADS * HEAD_DIM + (low - width) * 2 + c * HEAD_DIM
            both_sides.append(bias[:, start : start + HEAD_DIM].astype(jnp.float32))
        return jnp.where(core == 0, both_sides[0], both_sides[1])

    def side(s, carry):
        length = lens[serve[d - core + s]]
        turn = (length + slots).astype(jnp.float32) * inverse
        cos = jnp.cos(turn)
        sin = jnp.sin(turn)
        sin = jnp.where(flip, -sin, sin)
        cos = jnp.broadcast_to(cos[None], (TOK // SPAN, SPAN, HEAD_DIM)).reshape(TOK, HEAD_DIM)
        sin = jnp.broadcast_to(sin[None], (TOK // SPAN, SPAN, HEAD_DIM)).reshape(TOK, HEAD_DIM)
        for low in range(0, GW, 2 * HEAD_DIM):
            high = min(low + 2 * HEAD_DIM, GW)
            part = jnp.dot(normed[s], w_buf[:, low:high], preferred_element_type=jnp.float32)
            for u in range((high - low) // HEAD_DIM):
                head = part[:, u * HEAD_DIM : (u + 1) * HEAD_DIM] + bias_at(low + u * HEAD_DIM)
                index = low // HEAD_DIM + u
                if index <= GROUP:
                    head = head * cos + pltpu.roll(head, HEAD_DIM // 2, 1) * sin
                head = head.astype(jnp.bfloat16)
                if index < GROUP:
                    for t in range(TILES):
                        q_out[s, t, index * TILE : (index + 1) * TILE, :] = head[
                            t * TILE : (t + 1) * TILE
                        ]
                else:
                    col = (index - GROUP) * HEAD_DIM
                    own_out[s, :, col : col + HEAD_DIM] = head
        return carry

    lax.fori_loop(0, 2, side, 0)

    def finish(k, carry):
        y_copy(2, k, opposite).wait_recv()
        y_copy(3, k, opposite).wait_recv()
        y_copy(0, k, y).wait_send()
        y_copy(1, k, y).wait_send()
        y_copy(2, k, down).wait_send()
        y_copy(3, k, up).wait_send()
        return carry

    lax.fori_loop(0, 16, finish, 0)
    give_kv.wait_send()
    for dx, dz in sends[1:]:
        for c2 in range(2):
            outgoing(dx, dz, c2).wait_send()
    for _, copy in bouncing():
        copy.wait_send()
    for stage in range(5):
        for h in (0, 1):
            for kind in range(4):
                w_copy(h, stage, kind, w_row(h, stage, kind)).wait_send()
    give_w.wait_send()
    give_h.wait_send()


def communicate(lens, serve, kv, w, hidden, gain, bias):
    any_spec = pl.BlockSpec(memory_space=pl.ANY)
    vmem_spec = pl.BlockSpec(memory_space=pltpu.VMEM)
    smem_spec = pl.BlockSpec(memory_space=pltpu.SMEM)
    dma = pltpu.SemaphoreType.DMA
    return pl.pallas_call(
        exchange,
        out_shape=(
            jax.ShapeDtypeStruct((2, TILES, TQ, HEAD_DIM), jnp.bfloat16),
            jax.ShapeDtypeStruct((2, TOK, 2 * HEAD_DIM), jnp.bfloat16),
            jax.ShapeDtypeStruct((2, CAP, 2 * HEAD_DIM), jnp.bfloat16),
        ),
        in_specs=[smem_spec] * 2 + [vmem_spec] * 5,
        out_specs=(vmem_spec, vmem_spec, any_spec),
        scratch_shapes=[
            pltpu.VMEM((D, GW), jnp.bfloat16),
            pltpu.VMEM((2, STRIPE, GW), jnp.bfloat16),
            pltpu.VMEM((16, 2, 2, SLICE, 2 * HEAD_DIM), jnp.bfloat16),
            pltpu.VMEM((TOK, D), jnp.bfloat16),
            pltpu.VMEM((2, TOK, D), jnp.bfloat16),
            pltpu.VMEM((8, 2, SLICE, 2 * HEAD_DIM), jnp.bfloat16),
            dma((2,)),
            dma((2,)),
            dma((2,)),
            dma((16, 2)),
            dma((16, 2)),
            dma((8,)),
            dma((8,)),
            dma((4, 16)),
            dma((4, 16)),
            dma((2, 5, 4)),
            dma((2, 5, 4)),
        ],
        compiler_params=pltpu.CompilerParams(
            collective_id=0, has_side_effects=True, vmem_limit_bytes=VMEM_LIMIT
        ),
        name="exchange",
    )(lens, serve, kv, w, hidden, gain, bias)


def attend_kernel(lens, serve, q, own, kv, out, kv_buf, scores, sems):
    d = lax.axis_index("dp")
    first = d - lax.rem(d, 2)

    def extent(s):
        length = lens[serve[first + s]]
        return length, length // STEP, (length + STEP - 1) // STEP

    def load(s, j):
        rows = pl.ds(pl.multiple_of(j * STEP, STEP), STEP)
        return pltpu.make_async_copy(kv.at[s, rows, :], kv_buf.at[s, rows, :], sems.at[s, j])

    for s in range(2):

        def load_start(j, carry, s=s):
            load(s, j).start()
            return carry

        lax.fori_loop(0, extent(s)[2], load_start, 0)
    ones = jnp.ones((KB, 8), jnp.bfloat16)

    def tile(i, carry):
        s = i // TILES
        t = lax.rem(i, TILES)
        length, full, blocks = extent(s)
        query = q[s, t]

        def kv_rows(j):
            return pl.ds(pl.multiple_of(j * KB, KB), KB)

        def score(j, slot):
            scores[slot] = lax.dot_general(
                kv_buf[s, kv_rows(j), :HEAD_DIM],
                query,
                (((1,), (1,)), ((), ())),
                preferred_element_type=jnp.float32,
            )

        def absorb(state, raw, values, ones):
            top, acc = state
            new_top = jnp.maximum(top, jnp.max(raw, axis=0, keepdims=True))
            weights = jnp.exp2((raw - new_top) * FOLD).astype(jnp.bfloat16)
            factor = jnp.exp2((top - new_top) * FOLD)
            wide = jnp.concatenate([values, ones], axis=1)
            acc = acc * factor + lax.dot_general(
                wide, weights, (((0,), (0,)), ((), ())), preferred_element_type=jnp.float32
            )
            return new_top, acc

        def half(j, slot, state, masked):
            score(jnp.minimum(j + 1, 2 * blocks - 1), 1 - slot)
            raw = scores[slot]
            if masked:
                row = j * KB + lax.broadcasted_iota(jnp.int32, (KB, 1), 0)
                raw = jnp.where(row < length, raw, -jnp.inf)
            return absorb(state, raw, kv_buf[s, kv_rows(j), HEAD_DIM:], ones)

        def step(j, state, masked):
            @pl.when((t == 0) & (j + 1 < blocks))
            def _():
                load(s, j + 1).wait()

            state = half(2 * j, 0, state, masked)
            return half(2 * j + 1, 1, state, masked)

        own_rows = pl.ds(pl.multiple_of(t * TILE, TILE), TILE)
        raw = lax.dot_general(
            own[s, own_rows, :HEAD_DIM],
            query,
            (((1,), (1,)), ((), ())),
            preferred_element_type=jnp.float32,
        )
        key_id = lax.broadcasted_iota(jnp.int32, (TILE, TQ), 0)
        query_id = lax.rem(lax.broadcasted_iota(jnp.int32, (TILE, TQ), 1), TILE)
        seen = (key_id // SPAN == query_id // SPAN) & (key_id <= query_id)
        raw = jnp.where(seen, raw, -jnp.inf)
        state = (
            jnp.full((1, TQ), -jnp.inf, jnp.float32),
            jnp.zeros((HEAD_DIM + 8, TQ), jnp.float32),
        )
        state = absorb(state, raw, own[s, own_rows, HEAD_DIM:], ones[:TILE])

        @pl.when(t == 0)
        def _():
            load(s, 0).wait()

        score(0, 0)
        state = lax.fori_loop(0, full, lambda j, state: step(j, state, False), state)
        state = lax.fori_loop(full, blocks, lambda j, state: step(j, state, True), state)
        _, acc = state
        result = acc[:HEAD_DIM] / acc[HEAD_DIM : HEAD_DIM + 1]
        for h in range(GROUP):
            out[s, own_rows, h * HEAD_DIM : (h + 1) * HEAD_DIM] = result[
                :, h * TILE : (h + 1) * TILE
            ].T.astype(jnp.bfloat16)
        return carry

    lax.fori_loop(0, 2 * TILES, tile, 0)


def attend(lens, serve, q, own, kv):
    vmem_spec = pl.BlockSpec(memory_space=pltpu.VMEM)
    smem_spec = pl.BlockSpec(memory_space=pltpu.SMEM)
    return pl.pallas_call(
        attend_kernel,
        out_shape=jax.ShapeDtypeStruct((2, TOK, GROUP * HEAD_DIM), jnp.bfloat16),
        in_specs=[smem_spec, smem_spec, vmem_spec, vmem_spec, pl.BlockSpec(memory_space=pl.ANY)],
        out_specs=vmem_spec,
        scratch_shapes=[
            pltpu.VMEM((2, CAP, 2 * HEAD_DIM), jnp.bfloat16),
            pltpu.VMEM((2, KB, TQ), jnp.float32),
            pltpu.SemaphoreType.DMA((2, CAP // STEP)),
        ],
        compiler_params=pltpu.CompilerParams(vmem_limit_bytes=VMEM_LIMIT),
        name="attend",
    )(lens, serve, q, own, kv)


def swap_kernel(out, got, sems):
    y = lax.axis_index("grp")
    d = lax.axis_index("dp")
    core = lax.rem(d, 2)
    target = (y, d + 1 - 2 * core)
    barrier = pltpu.get_barrier_semaphore()
    pl.semaphore_signal(barrier, inc=1, device_id=target, device_id_type=MESH)
    pl.semaphore_wait(barrier, 1)
    copy = pltpu.make_async_remote_copy(
        src_ref=out.at[1 - core],
        dst_ref=got,
        send_sem=sems.at[0],
        recv_sem=sems.at[1],
        device_id=target,
        device_id_type=MESH,
    )
    copy.start()
    copy.wait()


def swap(out):
    vmem_spec = pl.BlockSpec(memory_space=pltpu.VMEM)
    return pl.pallas_call(
        swap_kernel,
        out_shape=jax.ShapeDtypeStruct((TOK, GROUP * HEAD_DIM), jnp.bfloat16),
        in_specs=[vmem_spec],
        out_specs=vmem_spec,
        scratch_shapes=[pltpu.SemaphoreType.DMA((2,))],
        compiler_params=pltpu.CompilerParams(collective_id=1, has_side_effects=True),
        name="swap",
    )(out)


def shards(hidden, norm_gain, w_qkv, qkv_bias, kv_cache, prompt_len, serve_prompt, resp_live):
    core = lax.axis_index("dp") % 2
    q, own, kv = communicate(
        prompt_len, serve_prompt, kv_cache, w_qkv, hidden, norm_gain[None, :], qkv_bias[None, :]
    )
    out = attend(prompt_len, serve_prompt, q, own, kv)
    far = swap(out)
    low = jnp.where(core == 0, out[0], far)
    high = jnp.where(core == 0, far, out[1])
    result = jnp.concatenate([low, high], axis=1)
    keep = (jnp.arange(SPAN, dtype=jnp.int32)[None, :] < resp_live[:, None]).reshape(TOK, 1)
    return jnp.where(keep, result, jnp.zeros((), jnp.bfloat16))


def solution(mesh):
    in_specs = (
        P(("grp", "dp"), None),
        P(),
        P("dp", None),
        P(),
        P(None, ("grp", "dp"), None),
        P(),
        P(),
        P(("grp", "dp")),
    )
    out_specs = P(("grp", "dp"), None)
    return jax.shard_map(shards, mesh=mesh, in_specs=in_specs, out_specs=out_specs, check_vma=False)
```

```python
import functools
import math

import jax
import jax.numpy as jnp
from jax import lax
from jax.experimental import pallas as pl
from jax.experimental.pallas import tpu as pltpu
from jax.sharding import PartitionSpec as P

D = 3584
HEADS = 14
GROUP = 7
HEAD_DIM = 128
SPAN = 16
CAP = 8192
TOK = 384
STRIPE = 112
GW = 1152
PLANE = 2048
SLICE = 64
TILE = 128
TQ = GROUP * TILE
TILES = TOK // TILE
KB = 512
STEP = 2 * KB
FIRST = 64
ROPE_BASE = 1000000.0
EPSILON = 1e-06
FOLD = math.log2(math.e) / math.sqrt(HEAD_DIM)
MESH = pl.DeviceIdType.MESH
OFFSETS = (0, 1, 3, 2)
NEAR = ((1, 0), (3, 0), (0, 1), (0, 3))
DIAGONAL = ((1, 1), (3, 3), (1, 3), (3, 1))
TIES = ((2, 1), (2, 3), (1, 2), (3, 2))
STRAIGHT = ((2, 0), (0, 2), (2, 2))
ORDER = ((0, 0),) + NEAR + DIAGONAL + STRAIGHT[:2] + TIES + STRAIGHT[2:]
VMEM_LIMIT = 64 * 1000 * 1000


def exchange(
    lens,
    serve,
    kv,
    w,
    hid,
    gain,
    bias,
    q_out,
    own_out,
    kv_out,
    w_buf,
    w_pack,
    kv_pack,
    hid_far,
    normed,
    bounce,
    local_sem,
    pair_send,
    pair_recv,
    kv_send,
    kv_recv,
    bounce_send,
    bounce_recv,
    y_send,
    y_recv,
    w_send,
    w_recv,
):
    y = lax.axis_index("grp")
    d = lax.axis_index("dp")
    core = lax.rem(d, 2)
    z = lax.rem(d // 2, 4)
    x = d // 8
    chip = d // 2
    up = lax.rem(y + 1, 4)
    down = lax.rem(y + 3, 4)
    opposite = lax.rem(y + 2, 4)
    partner = d + 1 - 2 * core

    barrier = pltpu.get_barrier_semaphore()

    def greet(k, carry):
        pl.semaphore_signal(
            barrier, inc=1, device_id=(y, lax.rem(d + k, 32)), device_id_type=MESH
        )
        return carry

    lax.fori_loop(1, 32, greet, 0)
    for other in (up, down):
        pl.semaphore_signal(barrier, inc=1, device_id=(other, d), device_id_type=MESH)

    width = GROUP * HEAD_DIM
    for c in range(2):
        base = HEADS * HEAD_DIM + c * HEAD_DIM
        w_pack[c, :, :width] = w[:, c * width : (c + 1) * width]
        w_pack[c, :, width : width + HEAD_DIM] = w[:, base : base + HEAD_DIM]
        w_pack[c, :, width + HEAD_DIM :] = w[:, base + 2 * HEAD_DIM : base + 3 * HEAD_DIM]

    def pack(j, carry):
        for p in range(2):
            rows = kv[serve[2 * j + p]]
            for c in range(2):
                for part in range(2):
                    col = (2 * part + c) * HEAD_DIM
                    kv_pack[j, c, p, :, part * HEAD_DIM : (part + 1) * HEAD_DIM] = rows[
                        :, col : col + HEAD_DIM
                    ]
        return carry

    lax.fori_loop(0, 16, pack, 0)
    pl.semaphore_wait(barrier, 33)

    def stripe(row, rows):
        return w_buf.at[pl.ds(pl.multiple_of(row, 16), rows), :]

    def remote(src, dst, send, recv, target):
        return pltpu.make_async_remote_copy(
            src_ref=src,
            dst_ref=dst,
            send_sem=send,
            recv_sem=recv,
            device_id=target,
            device_id_type=MESH,
        )

    def at(px, pz, pc):
        return lax.rem(px, 4) * 8 + lax.rem(pz, 4) * 2 + pc

    def kv_rows(plane, source):
        return pl.ds(pl.multiple_of(plane * PLANE + source * SLICE, SLICE), SLICE)

    my_row = d * STRIPE
    give_w = remote(
        w_pack.at[1 - core], stripe(my_row, STRIPE), pair_send.at[0], pair_recv.at[0], (y, partner)
    )
    give_w.start()
    take_w = remote(
        w_pack.at[1 - core],
        stripe(partner * STRIPE, STRIPE),
        pair_send.at[0],
        pair_recv.at[0],
        (y, partner),
    )
    keep_w = pltpu.make_async_copy(w_pack.at[core], stripe(my_row, STRIPE), local_sem.at[0])
    keep_w.start()
    keep_kv = pltpu.make_async_copy(
        kv_pack.at[chip, core], kv_out.at[:, kv_rows(y, d), :], local_sem.at[1]
    )
    keep_kv.start()

    def order(dx, dz):
        return ORDER.index((dx, dz))

    def kv_copy(k, cs, source, target):
        return remote(
            kv_pack.at[target // 2, lax.rem(target, 2)],
            kv_out.at[:, kv_rows(y, source), :],
            kv_send.at[k, lax.rem(target, 2)],
            kv_recv.at[k, cs],
            (y, target),
        )

    def bounce_in(slot, k, far, middle):
        return remote(
            kv_pack.at[far // 2, lax.rem(far, 2)],
            bounce.at[slot],
            kv_send.at[k, lax.rem(far, 2)],
            bounce_recv.at[slot],
            (y, middle),
        )

    def bounce_out(slot, k, cs, source, target):
        return remote(
            bounce.at[slot],
            kv_out.at[:, kv_rows(y, source), :],
            bounce_send.at[slot],
            kv_recv.at[k, cs],
            (y, target),
        )

    def outgoing(dx, dz, c2):
        k = order(dx, dz)
        far = at(x + dx, z + dz, c2)
        if dx == 2 and dz % 2 == 1:
            return bounce_in(dz // 2 * 2 + core, k, far, at(x + 3, z + dz, c2))
        if dz == 2 and dx % 2 == 1:
            return bounce_in(4 + dx // 2 * 2 + core, k, far, at(x + dx, z + 3, c2))
        return kv_copy(k, core, d, far)

    def bouncing():
        for i, step in enumerate((1, 3)):
            for cs in range(2):
                slot = 2 * i + cs
                source = at(x + 1, z + 4 - step, cs)
                yield slot, bounce_out(slot, order(2, step), cs, source, at(x + 3, z, core))
                slot = 4 + 2 * i + cs
                source = at(x + 4 - step, z + 1, cs)
                yield slot, bounce_out(slot, order(step, 2), cs, source, at(x, z + 3, core))

    give_kv = kv_copy(0, core, d, partner)

    def issue(group):
        for dx, dz in group:
            for c2 in range(2):
                outgoing(dx, dz, c2).start()

    def place(h, first, second):
        if h == 0:
            return (lax.rem(first, 4) * 8 + lax.rem(second, 4) * 2) * STRIPE
        return (lax.rem(second, 4) * 8 + lax.rem(first, 4) * 2 + 1) * STRIPE

    def along(h, phase, shift):
        if (h == 0) == (phase == 1):
            return (y, at(x + shift, z, core))
        return (y, at(x, z + shift, core))

    def mine(h):
        return (x, z) if h == 0 else (z, x)

    def w_block(kind, row):
        if kind == 2:
            return stripe(row, FIRST)
        if kind == 3:
            return stripe(row + FIRST, STRIPE - FIRST)
        return stripe(row, STRIPE)

    def w_copy(h, stage, kind, row):
        phase = 1 if stage == 0 else 2
        shift = 1 if kind in (0, 2) else 3
        ref = w_block(kind, row)
        return remote(
            ref, ref, w_send.at[h, stage, kind], w_recv.at[h, stage, kind], along(h, phase, shift)
        )

    def w_row(h, stage, kind):
        first, second = mine(h)
        back = (3, 1, 2, 2)[kind]
        if stage == 0:
            return place(h, first + back, second)
        return place(h, first + OFFSETS[stage - 1], second + back)

    def w_wait(stage, kinds):
        for h in (0, 1):
            for kind in kinds:
                w_copy(h, stage, kind, w_row(h, stage, kind)).wait_recv()

    def w_start(stage):
        for h in (0, 1):
            first, second = mine(h)
            row = place(h, first, second)
            if stage > 0:
                row = place(h, first + OFFSETS[stage - 1], second)
            for kind in (0, 1):
                w_copy(h, stage, kind, row).start()

    def w_forward(stage):
        for h in (0, 1):
            for kind in (0, 1):
                w_copy(h, stage, kind + 2, w_row(h, stage, kind)).start()

    give_h = remote(hid, hid_far, pair_send.at[1], pair_recv.at[1], (y, partner))

    def chip_of(k):
        dx, dz = ORDER[k]
        return lax.rem(x + 4 - dx, 4) * 4 + lax.rem(z + 4 - dz, 4)

    def chip_rows(plane, k):
        return pl.ds(pl.multiple_of(plane * PLANE + chip_of(k) * 2 * SLICE, SLICE), 2 * SLICE)

    def y_copy(kind, k, plane):
        rows = chip_rows(plane, k)
        if kind >= 2:
            ref = kv_out.at[kind - 2, rows, :]
        else:
            ref = kv_out.at[:, rows, :]
        target = (up, d) if kind in (0, 2) else (down, d)
        return remote(ref, ref, y_send.at[kind, k], y_recv.at[kind, k], target)

    def spread(k):
        for cs in range(2):
            kv_copy(k, cs, chip_of(k) * 2 + cs, d).wait_recv()
        y_copy(0, k, y).start()
        y_copy(1, k, y).start()

    def relay(k):
        y_copy(0, k, down).wait_recv()
        y_copy(2, k, down).start()
        y_copy(1, k, up).wait_recv()
        y_copy(3, k, up).start()

    def norm(source, slot):
        scale = gain[...].astype(jnp.float32).reshape(1, D)

        def rows(i, carry):
            part = pl.ds(pl.multiple_of(i * 32, 32), 32)
            values = source[part, :].astype(jnp.float32)
            spread = lax.rsqrt(jnp.mean(values * values, axis=-1, keepdims=True) + EPSILON)
            scaled = values * spread * scale
            normed[slot, part, :] = scaled.astype(jnp.bfloat16)
            return carry

        lax.fori_loop(0, TOK // 32, rows, 0)

    def first_spread():
        keep_kv.wait()
        kv_copy(0, 1 - core, partner, d).wait_recv()
        y_copy(0, 0, y).start()
        y_copy(1, 0, y).start()

    def begin_w():
        keep_w.wait()
        take_w.wait_recv()
        w_start(0)

    def hop(stage):
        w_wait(stage, (0, 1))
        w_forward(stage)

    def bounce_all():
        for slot, copy in bouncing():
            bounce_in(slot, 0, d, d).wait_recv()
            copy.start()

    def norm_far():
        give_h.wait_recv()
        norm(hid_far, 1 - core)

    give_kv.start()
    issue(NEAR)
    issue(DIAGONAL)
    issue(TIES)
    begin_w()
    issue(STRAIGHT)
    give_h.start()
    first_spread()
    for k in range(1, 5):
        spread(k)
    bounce_all()
    for k in range(5, 9):
        spread(k)
    hop(0)
    w_start(1)
    for k in range(9, 12):
        spread(k)
    w_start(2)
    w_start(3)
    norm(hid, core)
    for k in range(12, 16):
        spread(k)
        relay(k - 12)
    for k in range(4, 6):
        relay(k)
    hop(1)
    norm_far()
    for k in range(6, 12):
        relay(k)
    w_wait(0, (2, 3))
    w_start(4)
    hop(2)
    for k in range(12, 16):
        relay(k)
    hop(3)
    hop(4)
    for stage in (1, 2, 3, 4):
        w_wait(stage, (2, 3))

    steps_range = lax.broadcasted_iota(jnp.int32, (SPAN, HEAD_DIM), 1)
    steps_range = jnp.where(
        steps_range < HEAD_DIM // 2, steps_range, steps_range - HEAD_DIM // 2
    ).astype(jnp.float32)
    inverse = jnp.exp(steps_range * (-2.0 * math.log(ROPE_BASE) / HEAD_DIM))
    flip = lax.broadcasted_iota(jnp.int32, (SPAN, HEAD_DIM), 1) < HEAD_DIM // 2
    slots = lax.broadcasted_iota(jnp.int32, (SPAN, HEAD_DIM), 0)

    bias_row = bias[...].astype(jnp.float32).reshape(1, 2 * GW)

    def bias_at(low):
        both_sides = []
        for c in range(2):
            start = c * width + low
            if low >= width:
                start = HEADS * HEAD_DIM + (low - width) * 2 + c * HEAD_DIM
            both_sides.append(bias_row[:, start : start + HEAD_DIM])
        return jnp.where(core == 0, both_sides[0], both_sides[1])

    def side(s, carry):
        length = lens[serve[d - core + s]]
        turn = (length + slots).astype(jnp.float32) * inverse
        cos = jnp.cos(turn)
        sin = jnp.sin(turn)
        sin = jnp.where(flip, -sin, sin)
        cos = jnp.broadcast_to(cos[None], (TOK // SPAN, SPAN, HEAD_DIM)).reshape(TOK, HEAD_DIM)
        sin = jnp.broadcast_to(sin[None], (TOK // SPAN, SPAN, HEAD_DIM)).reshape(TOK, HEAD_DIM)
        for low in range(0, GW, 2 * HEAD_DIM):
            high = min(low + 2 * HEAD_DIM, GW)
            part = jnp.dot(normed[s], w_buf[:, low:high], preferred_element_type=jnp.float32)
            for u in range((high - low) // HEAD_DIM):
                head = part[:, u * HEAD_DIM : (u + 1) * HEAD_DIM] + bias_at(low + u * HEAD_DIM)
                index = low // HEAD_DIM + u
                if index <= GROUP:
                    head = head * cos + pltpu.roll(head, HEAD_DIM // 2, 1) * sin
                head = head.astype(jnp.bfloat16)
                if index < GROUP:
                    for t in range(TILES):
                        q_out[s, t, index * TILE : (index + 1) * TILE, :] = head[
                            t * TILE : (t + 1) * TILE
                        ]
                else:
                    col = (index - GROUP) * HEAD_DIM
                    own_out[s, :, col : col + HEAD_DIM] = head
        return carry

    lax.fori_loop(0, 2, side, 0)

    for k in range(16):
        y_copy(2, k, opposite).wait_recv()
        y_copy(3, k, opposite).wait_recv()
        y_copy(0, k, y).wait_send()
        y_copy(1, k, y).wait_send()
        y_copy(2, k, down).wait_send()
        y_copy(3, k, up).wait_send()
    give_kv.wait_send()
    for dx, dz in ORDER[1:]:
        for c2 in range(2):
            outgoing(dx, dz, c2).wait_send()
    for _, copy in bouncing():
        copy.wait_send()
    for stage in range(5):
        for h in (0, 1):
            for kind in range(4):
                w_copy(h, stage, kind, w_row(h, stage, kind)).wait_send()
    give_w.wait_send()
    give_h.wait_send()


def communicate(lens, serve, kv, w, hidden, gain, bias):
    any_spec = pl.BlockSpec(memory_space=pl.ANY)
    vmem_spec = pl.BlockSpec(memory_space=pltpu.VMEM)
    smem_spec = pl.BlockSpec(memory_space=pltpu.SMEM)
    dma = pltpu.SemaphoreType.DMA
    return pl.pallas_call(
        exchange,
        out_shape=(
            jax.ShapeDtypeStruct((2, TILES, TQ, HEAD_DIM), jnp.bfloat16),
            jax.ShapeDtypeStruct((2, TOK, 2 * HEAD_DIM), jnp.bfloat16),
            jax.ShapeDtypeStruct((2, CAP, 2 * HEAD_DIM), jnp.bfloat16),
        ),
        in_specs=[smem_spec] * 2 + [vmem_spec] * 5,
        out_specs=(vmem_spec, vmem_spec, any_spec),
        scratch_shapes=[
            pltpu.VMEM((D, GW), jnp.bfloat16),
            pltpu.VMEM((2, STRIPE, GW), jnp.bfloat16),
            pltpu.VMEM((16, 2, 2, SLICE, 2 * HEAD_DIM), jnp.bfloat16),
            pltpu.VMEM((TOK, D), jnp.bfloat16),
            pltpu.VMEM((2, TOK, D), jnp.bfloat16),
            pltpu.VMEM((8, 2, SLICE, 2 * HEAD_DIM), jnp.bfloat16),
            dma((2,)),
            dma((2,)),
            dma((2,)),
            dma((16, 2)),
            dma((16, 2)),
            dma((8,)),
            dma((8,)),
            dma((4, 16)),
            dma((4, 16)),
            dma((2, 5, 4)),
            dma((2, 5, 4)),
        ],
        compiler_params=pltpu.CompilerParams(
            collective_id=0, has_side_effects=True, vmem_limit_bytes=VMEM_LIMIT
        ),
        name="exchange",
    )(lens, serve, kv, w, hidden, gain, bias)


def attend_kernel(lens, serve, q, own, kv, out, kv_buf, scores, sems):
    d = lax.axis_index("dp")
    first = d - lax.rem(d, 2)

    def extent(s):
        length = lens[serve[first + s]]
        return length, length // STEP, (length + STEP - 1) // STEP

    def load(s, j):
        rows = pl.ds(pl.multiple_of(j * STEP, STEP), STEP)
        return pltpu.make_async_copy(kv.at[s, rows, :], kv_buf.at[s, rows, :], sems.at[s, j])

    for s in range(2):

        def load_start(j, carry, s=s):
            load(s, j).start()
            return carry

        lax.fori_loop(0, extent(s)[2], load_start, 0)
    ones = jnp.ones((KB, 8), jnp.bfloat16)
    key_id = lax.broadcasted_iota(jnp.int32, (TILE, TQ), 0)
    query_id = lax.rem(lax.broadcasted_iota(jnp.int32, (TILE, TQ), 1), TILE)
    seen = (key_id // SPAN == query_id // SPAN) & (key_id <= query_id)

    def tile(i, carry):
        s = i // TILES
        t = lax.rem(i, TILES)
        length, full, blocks = extent(s)
        query = q[s, t]

        def kv_rows(j):
            return pl.ds(pl.multiple_of(j * KB, KB), KB)

        def score(j, slot, masked):
            raw = lax.dot_general(
                kv_buf[s, kv_rows(j), :HEAD_DIM],
                query,
                (((1,), (1,)), ((), ())),
                preferred_element_type=jnp.float32,
            )
            if masked:
                row = j * KB + lax.broadcasted_iota(jnp.int32, (KB, 1), 0)
                raw = jnp.where(row < length, raw, -jnp.inf)
            scores[slot] = raw
            return jnp.max(raw, axis=0, keepdims=True)

        def absorb(state, raw, peak, values, ones):
            top, acc = state
            new_top = jnp.maximum(top, peak)
            weights = jnp.exp2((raw - new_top) * FOLD).astype(jnp.bfloat16)
            factor = jnp.exp2((top - new_top) * FOLD)
            wide = jnp.concatenate([values, ones], axis=1)
            acc = acc * factor + lax.dot_general(
                wide, weights, (((0,), (0,)), ((), ())), preferred_element_type=jnp.float32
            )
            return new_top, acc

        def step(j, carry, masked):
            peak, state = carry

            @pl.when((t == 0) & (j + 1 < blocks))
            def _():
                load(s, j + 1).wait()

            ahead = score(2 * j + 1, 1, masked)
            state = absorb(state, scores[0], peak, kv_buf[s, kv_rows(2 * j), HEAD_DIM:], ones)
            peak = score(jnp.minimum(2 * j + 2, 2 * blocks - 1), 0, masked)
            state = absorb(state, scores[1], ahead, kv_buf[s, kv_rows(2 * j + 1), HEAD_DIM:], ones)
            return peak, state

        @pl.when(t == 0)
        def _():
            load(s, 0).wait()

        own_rows = pl.ds(pl.multiple_of(t * TILE, TILE), TILE)
        raw = lax.dot_general(
            own[s, own_rows, :HEAD_DIM],
            query,
            (((1,), (1,)), ((), ())),
            preferred_element_type=jnp.float32,
        )
        peak = score(0, 0, False)
        raw = jnp.where(seen, raw, -jnp.inf)
        state = (
            jnp.full((1, TQ), -jnp.inf, jnp.float32),
            jnp.zeros((HEAD_DIM + 8, TQ), jnp.float32),
        )
        state = absorb(
            state, raw, jnp.max(raw, axis=0, keepdims=True), own[s, own_rows, HEAD_DIM:], ones[:TILE]
        )
        near = jnp.where(full == blocks, full, full - 1)
        work = lax.fori_loop(0, near, lambda j, c: step(j, c, False), (peak, state))
        _, state = lax.fori_loop(near, blocks, lambda j, c: step(j, c, True), work)
        _, acc = state
        result = (acc[:HEAD_DIM] * (1.0 / acc[HEAD_DIM : HEAD_DIM + 1])).astype(jnp.bfloat16)
        for h in range(GROUP):
            out[s, own_rows, h * HEAD_DIM : (h + 1) * HEAD_DIM] = result[
                :, h * TILE : (h + 1) * TILE
            ].T
        return carry

    lax.fori_loop(0, 2 * TILES, tile, 0)


def attend(lens, serve, q, own, kv):
    vmem_spec = pl.BlockSpec(memory_space=pltpu.VMEM)
    smem_spec = pl.BlockSpec(memory_space=pltpu.SMEM)
    return pl.pallas_call(
        attend_kernel,
        out_shape=jax.ShapeDtypeStruct((2, TOK, GROUP * HEAD_DIM), jnp.bfloat16),
        in_specs=[smem_spec, smem_spec, vmem_spec, vmem_spec, pl.BlockSpec(memory_space=pl.ANY)],
        out_specs=vmem_spec,
        scratch_shapes=[
            pltpu.VMEM((2, CAP, 2 * HEAD_DIM), jnp.bfloat16),
            pltpu.VMEM((2, KB, TQ), jnp.float32),
            pltpu.SemaphoreType.DMA((2, CAP // STEP)),
        ],
        compiler_params=pltpu.CompilerParams(vmem_limit_bytes=VMEM_LIMIT),
        name="attend",
    )(lens, serve, q, own, kv)


def swap_kernel(live, out, result, got, sems):
    y = lax.axis_index("grp")
    d = lax.axis_index("dp")
    core = lax.rem(d, 2)
    target = (y, d + 1 - 2 * core)
    barrier = pltpu.get_barrier_semaphore()
    pl.semaphore_signal(barrier, inc=1, device_id=target, device_id_type=MESH)
    pl.semaphore_wait(barrier, 1)
    copy = pltpu.make_async_remote_copy(
        src_ref=out.at[1 - core],
        dst_ref=got,
        send_sem=sems.at[0],
        recv_sem=sems.at[1],
        device_id=target,
        device_id_type=MESH,
    )
    copy.start()
    width = GROUP * HEAD_DIM
    slot = lax.broadcasted_iota(jnp.int32, (SPAN, width), 0)

    def fill(source, side):
        cols = pl.ds(pl.multiple_of(side * width, HEAD_DIM), width)

        def rows(r, carry):
            part = pl.ds(pl.multiple_of(r * SPAN, SPAN), SPAN)
            values = source[part, :].astype(jnp.float32)
            result[part, cols] = jnp.where(slot < live[r], values, 0.0).astype(jnp.bfloat16)
            return carry

        lax.fori_loop(0, TOK // SPAN, rows, 0)

    fill(out.at[core], core)
    copy.wait()
    fill(got, 1 - core)


def swap(live, out):
    vmem_spec = pl.BlockSpec(memory_space=pltpu.VMEM)
    return pl.pallas_call(
        swap_kernel,
        out_shape=jax.ShapeDtypeStruct((TOK, 2 * GROUP * HEAD_DIM), jnp.bfloat16),
        in_specs=[pl.BlockSpec(memory_space=pltpu.SMEM), vmem_spec],
        out_specs=vmem_spec,
        scratch_shapes=[
            pltpu.VMEM((TOK, GROUP * HEAD_DIM), jnp.bfloat16),
            pltpu.SemaphoreType.DMA((2,)),
        ],
        compiler_params=pltpu.CompilerParams(collective_id=1, has_side_effects=True),
        name="swap",
    )(live, out)


def shards(hidden, norm_gain, w_qkv, qkv_bias, kv_cache, prompt_len, serve_prompt, resp_live):
    q, own, kv = communicate(
        prompt_len, serve_prompt, kv_cache, w_qkv, hidden, norm_gain, qkv_bias
    )
    out = attend(prompt_len, serve_prompt, q, own, kv)
    return swap(resp_live, out)


def solution(mesh):
    in_specs = (
        P(("grp", "dp"), None),
        P(),
        P("dp", None),
        P(),
        P(None, ("grp", "dp"), None),
        P(),
        P(),
        P(("grp", "dp")),
    )
    out_specs = P(("grp", "dp"), None)
    return jax.shard_map(shards, mesh=mesh, in_specs=in_specs, out_specs=out_specs, check_vma=False)
```

```python
import functools
import math

import jax
import jax.numpy as jnp
from jax import lax
from jax.experimental import pallas as pl
from jax.experimental.pallas import tpu as pltpu
from jax.sharding import PartitionSpec as P

D = 3584
HEADS = 14
GROUP = 7
HEAD_DIM = 128
SPAN = 16
CAP = 8192
TOK = 384
STRIPE = 112
GW = 1152
PLANE = 2048
SLICE = 64
TILE = 128
TQ = GROUP * TILE
TILES = TOK // TILE
KB = 512
STEP = 2 * KB
FIRST = 64
ROPE_BASE = 1000000.0
EPSILON = 1e-06
FOLD = math.log2(math.e) / math.sqrt(HEAD_DIM)
MESH = pl.DeviceIdType.MESH
OFFSETS = (0, 1, 3, 2)
NEAR = ((1, 0), (3, 0), (0, 1), (0, 3))
DIAGONAL = ((1, 1), (3, 3), (1, 3), (3, 1))
TIES = ((2, 1), (2, 3), (1, 2), (3, 2))
STRAIGHT = ((2, 0), (0, 2), (2, 2))
ORDER = ((0, 0),) + NEAR + DIAGONAL + STRAIGHT[:2] + TIES + STRAIGHT[2:]
VMEM_LIMIT = 64 * 1000 * 1000


def exchange(
    lens,
    serve,
    kv_in,
    w_in,
    hid_in,
    gain,
    bias,
    q_out,
    own_out,
    kv_out,
    kv,
    w,
    hid,
    w_buf,
    w_pack,
    kv_pack,
    hid_far,
    normed,
    bounce,
    local_sem,
    pair_send,
    pair_recv,
    kv_send,
    kv_recv,
    bounce_send,
    bounce_recv,
    y_send,
    y_recv,
    w_send,
    w_recv,
):
    y = lax.axis_index("grp")
    d = lax.axis_index("dp")
    core = lax.rem(d, 2)
    z = lax.rem(d // 2, 4)
    x = d // 8
    chip = d // 2
    up = lax.rem(y + 1, 4)
    down = lax.rem(y + 3, 4)
    opposite = lax.rem(y + 2, 4)
    partner = d + 1 - 2 * core

    fetch = [
        pltpu.make_async_copy(w_in, w, local_sem.at[2]),
        pltpu.make_async_copy(kv_in, kv, local_sem.at[3]),
        pltpu.make_async_copy(hid_in, hid, local_sem.at[4]),
    ]
    for copy in fetch:
        copy.start()
    barrier = pltpu.get_barrier_semaphore()

    def greet(k, carry):
        pl.semaphore_signal(
            barrier, inc=1, device_id=(y, lax.rem(d + k, 32)), device_id_type=MESH
        )
        return carry

    lax.fori_loop(1, 32, greet, 0)
    for other in (up, down):
        pl.semaphore_signal(barrier, inc=1, device_id=(other, d), device_id_type=MESH)

    width = GROUP * HEAD_DIM
    fetch[0].wait()
    for c in range(2):
        base = HEADS * HEAD_DIM + c * HEAD_DIM
        w_pack[c, :, :width] = w[:, c * width : (c + 1) * width]
        w_pack[c, :, width : width + HEAD_DIM] = w[:, base : base + HEAD_DIM]
        w_pack[c, :, width + HEAD_DIM :] = w[:, base + 2 * HEAD_DIM : base + 3 * HEAD_DIM]

    def pack(j, carry):
        for p in range(2):
            rows = kv[serve[2 * j + p]]
            for c in range(2):
                for part in range(2):
                    col = (2 * part + c) * HEAD_DIM
                    kv_pack[j, c, p, :, part * HEAD_DIM : (part + 1) * HEAD_DIM] = rows[
                        :, col : col + HEAD_DIM
                    ]
        return carry

    fetch[1].wait()
    lax.fori_loop(0, 16, pack, 0)
    fetch[2].wait()
    pl.semaphore_wait(barrier, 33)

    def stripe(row, rows):
        return w_buf.at[pl.ds(pl.multiple_of(row, 16), rows), :]

    def remote(src, dst, send, recv, target):
        return pltpu.make_async_remote_copy(
            src_ref=src,
            dst_ref=dst,
            send_sem=send,
            recv_sem=recv,
            device_id=target,
            device_id_type=MESH,
        )

    def at(px, pz, pc):
        return lax.rem(px, 4) * 8 + lax.rem(pz, 4) * 2 + pc

    def kv_rows(plane, source):
        return pl.ds(pl.multiple_of(plane * PLANE + source * SLICE, SLICE), SLICE)

    my_row = d * STRIPE
    give_w = remote(
        w_pack.at[1 - core], stripe(my_row, STRIPE), pair_send.at[0], pair_recv.at[0], (y, partner)
    )
    give_w.start()
    take_w = remote(
        w_pack.at[1 - core],
        stripe(partner * STRIPE, STRIPE),
        pair_send.at[0],
        pair_recv.at[0],
        (y, partner),
    )
    keep_w = pltpu.make_async_copy(w_pack.at[core], stripe(my_row, STRIPE), local_sem.at[0])
    keep_w.start()
    keep_kv = pltpu.make_async_copy(
        kv_pack.at[chip, core], kv_out.at[:, kv_rows(y, d), :], local_sem.at[1]
    )
    keep_kv.start()

    def order(dx, dz):
        return ORDER.index((dx, dz))

    def kv_copy(k, cs, source, target):
        return remote(
            kv_pack.at[target // 2, lax.rem(target, 2)],
            kv_out.at[:, kv_rows(y, source), :],
            kv_send.at[k, lax.rem(target, 2)],
            kv_recv.at[k, cs],
            (y, target),
        )

    def bounce_in(slot, k, far, middle):
        return remote(
            kv_pack.at[far // 2, lax.rem(far, 2)],
            bounce.at[slot],
            kv_send.at[k, lax.rem(far, 2)],
            bounce_recv.at[slot],
            (y, middle),
        )

    def bounce_out(slot, k, cs, source, target):
        return remote(
            bounce.at[slot],
            kv_out.at[:, kv_rows(y, source), :],
            bounce_send.at[slot],
            kv_recv.at[k, cs],
            (y, target),
        )

    def outgoing(dx, dz, c2):
        k = order(dx, dz)
        far = at(x + dx, z + dz, c2)
        if dx == 2 and dz % 2 == 1:
            return bounce_in(dz // 2 * 2 + core, k, far, at(x + 3, z + dz, c2))
        if dz == 2 and dx % 2 == 1:
            return bounce_in(4 + dx // 2 * 2 + core, k, far, at(x + dx, z + 3, c2))
        return kv_copy(k, core, d, far)

    def bouncing():
        for i, step in enumerate((1, 3)):
            for cs in range(2):
                slot = 2 * i + cs
                source = at(x + 1, z + 4 - step, cs)
                yield slot, bounce_out(slot, order(2, step), cs, source, at(x + 3, z, core))
                slot = 4 + 2 * i + cs
                source = at(x + 4 - step, z + 1, cs)
                yield slot, bounce_out(slot, order(step, 2), cs, source, at(x, z + 3, core))

    give_kv = kv_copy(0, core, d, partner)

    def issue(group):
        for dx, dz in group:
            for c2 in range(2):
                outgoing(dx, dz, c2).start()

    def place(h, first, second):
        if h == 0:
            return (lax.rem(first, 4) * 8 + lax.rem(second, 4) * 2) * STRIPE
        return (lax.rem(second, 4) * 8 + lax.rem(first, 4) * 2 + 1) * STRIPE

    def along(h, phase, shift):
        if (h == 0) == (phase == 1):
            return (y, at(x + shift, z, core))
        return (y, at(x, z + shift, core))

    def mine(h):
        return (x, z) if h == 0 else (z, x)

    def w_block(kind, row):
        if kind == 2:
            return stripe(row, FIRST)
        if kind == 3:
            return stripe(row + FIRST, STRIPE - FIRST)
        return stripe(row, STRIPE)

    def w_copy(h, stage, kind, row):
        phase = 1 if stage == 0 else 2
        shift = 1 if kind in (0, 2) else 3
        ref = w_block(kind, row)
        return remote(
            ref, ref, w_send.at[h, stage, kind], w_recv.at[h, stage, kind], along(h, phase, shift)
        )

    def w_row(h, stage, kind):
        first, second = mine(h)
        back = (3, 1, 2, 2)[kind]
        if stage == 0:
            return place(h, first + back, second)
        return place(h, first + OFFSETS[stage - 1], second + back)

    def w_wait(stage, kinds):
        for h in (0, 1):
            for kind in kinds:
                w_copy(h, stage, kind, w_row(h, stage, kind)).wait_recv()

    def w_start(stage):
        for h in (0, 1):
            first, second = mine(h)
            row = place(h, first, second)
            if stage > 0:
                row = place(h, first + OFFSETS[stage - 1], second)
            for kind in (0, 1):
                w_copy(h, stage, kind, row).start()

    def w_forward(stage):
        for h in (0, 1):
            for kind in (0, 1):
                w_copy(h, stage, kind + 2, w_row(h, stage, kind)).start()

    give_h = remote(hid, hid_far, pair_send.at[1], pair_recv.at[1], (y, partner))

    def chip_of(k):
        dx, dz = ORDER[k]
        return lax.rem(x + 4 - dx, 4) * 4 + lax.rem(z + 4 - dz, 4)

    def chip_rows(plane, k):
        return pl.ds(pl.multiple_of(plane * PLANE + chip_of(k) * 2 * SLICE, SLICE), 2 * SLICE)

    def y_copy(kind, k, plane):
        rows = chip_rows(plane, k)
        if kind >= 2:
            ref = kv_out.at[kind - 2, rows, :]
        else:
            ref = kv_out.at[:, rows, :]
        target = (up, d) if kind in (0, 2) else (down, d)
        return remote(ref, ref, y_send.at[kind, k], y_recv.at[kind, k], target)

    def spread(k):
        for cs in range(2):
            kv_copy(k, cs, chip_of(k) * 2 + cs, d).wait_recv()
        y_copy(0, k, y).start()
        y_copy(1, k, y).start()

    def relay(k):
        y_copy(0, k, down).wait_recv()
        y_copy(2, k, down).start()
        y_copy(1, k, up).wait_recv()
        y_copy(3, k, up).start()

    def norm(source, slot):
        scale = gain[...].astype(jnp.float32).reshape(1, D)

        def rows(i, carry):
            part = pl.ds(pl.multiple_of(i * 32, 32), 32)
            values = source[part, :].astype(jnp.float32)
            spread = lax.rsqrt(jnp.mean(values * values, axis=-1, keepdims=True) + EPSILON)
            scaled = values * spread * scale
            normed[slot, part, :] = scaled.astype(jnp.bfloat16)
            return carry

        lax.fori_loop(0, TOK // 32, rows, 0)

    def first_spread():
        keep_kv.wait()
        kv_copy(0, 1 - core, partner, d).wait_recv()
        y_copy(0, 0, y).start()
        y_copy(1, 0, y).start()

    def begin_w():
        keep_w.wait()
        take_w.wait_recv()
        w_start(0)

    def hop(stage):
        w_wait(stage, (0, 1))
        w_forward(stage)

    def bounce_all():
        for slot, copy in bouncing():
            bounce_in(slot, 0, d, d).wait_recv()
            copy.start()

    def norm_far():
        give_h.wait_recv()
        norm(hid_far, 1 - core)

    give_kv.start()
    issue(NEAR)
    issue(DIAGONAL)
    issue(TIES)
    begin_w()
    issue(STRAIGHT)
    give_h.start()
    first_spread()
    for k in range(1, 5):
        spread(k)
    bounce_all()
    for k in range(5, 9):
        spread(k)
    hop(0)
    w_start(1)
    for k in range(9, 12):
        spread(k)
    w_start(2)
    w_start(3)
    norm(hid, core)
    for k in range(12, 16):
        spread(k)
        relay(k - 12)
    for k in range(4, 6):
        relay(k)
    hop(1)
    norm_far()
    for k in range(6, 12):
        relay(k)
    w_wait(0, (2, 3))
    w_start(4)
    hop(2)
    for k in range(12, 16):
        relay(k)
    hop(3)
    hop(4)
    for stage in (1, 2, 3, 4):
        w_wait(stage, (2, 3))

    steps_range = lax.broadcasted_iota(jnp.int32, (SPAN, HEAD_DIM), 1)
    steps_range = jnp.where(
        steps_range < HEAD_DIM // 2, steps_range, steps_range - HEAD_DIM // 2
    ).astype(jnp.float32)
    inverse = jnp.exp(steps_range * (-2.0 * math.log(ROPE_BASE) / HEAD_DIM))
    flip = lax.broadcasted_iota(jnp.int32, (SPAN, HEAD_DIM), 1) < HEAD_DIM // 2
    slots = lax.broadcasted_iota(jnp.int32, (SPAN, HEAD_DIM), 0)

    bias_row = bias[...].astype(jnp.float32).reshape(1, 2 * GW)

    def bias_at(low):
        both_sides = []
        for c in range(2):
            start = c * width + low
            if low >= width:
                start = HEADS * HEAD_DIM + (low - width) * 2 + c * HEAD_DIM
            both_sides.append(bias_row[:, start : start + HEAD_DIM])
        return jnp.where(core == 0, both_sides[0], both_sides[1])

    def side(s, carry):
        length = lens[serve[d - core + s]]
        turn = (length + slots).astype(jnp.float32) * inverse
        cos = jnp.cos(turn)
        sin = jnp.sin(turn)
        sin = jnp.where(flip, -sin, sin)
        cos = jnp.broadcast_to(cos[None], (TOK // SPAN, SPAN, HEAD_DIM)).reshape(TOK, HEAD_DIM)
        sin = jnp.broadcast_to(sin[None], (TOK // SPAN, SPAN, HEAD_DIM)).reshape(TOK, HEAD_DIM)
        for low in range(0, GW, 2 * HEAD_DIM):
            high = min(low + 2 * HEAD_DIM, GW)
            part = jnp.dot(normed[s], w_buf[:, low:high], preferred_element_type=jnp.float32)
            for u in range((high - low) // HEAD_DIM):
                head = part[:, u * HEAD_DIM : (u + 1) * HEAD_DIM] + bias_at(low + u * HEAD_DIM)
                index = low // HEAD_DIM + u
                if index <= GROUP:
                    head = head * cos + pltpu.roll(head, HEAD_DIM // 2, 1) * sin
                head = head.astype(jnp.bfloat16)
                if index < GROUP:
                    for t in range(TILES):
                        q_out[s, t, index * TILE : (index + 1) * TILE, :] = head[
                            t * TILE : (t + 1) * TILE
                        ]
                else:
                    col = (index - GROUP) * HEAD_DIM
                    own_out[s, :, col : col + HEAD_DIM] = head
        return carry

    lax.fori_loop(0, 2, side, 0)

    for k in range(16):
        y_copy(2, k, opposite).wait_recv()
        y_copy(3, k, opposite).wait_recv()
        y_copy(0, k, y).wait_send()
        y_copy(1, k, y).wait_send()
        y_copy(2, k, down).wait_send()
        y_copy(3, k, up).wait_send()
    give_kv.wait_send()
    for dx, dz in ORDER[1:]:
        for c2 in range(2):
            outgoing(dx, dz, c2).wait_send()
    for _, copy in bouncing():
        copy.wait_send()
    for stage in range(5):
        for h in (0, 1):
            for kind in range(4):
                w_copy(h, stage, kind, w_row(h, stage, kind)).wait_send()
    give_w.wait_send()
    give_h.wait_send()


def communicate(lens, serve, kv, w, hidden, gain, bias):
    any_spec = pl.BlockSpec(memory_space=pl.ANY)
    vmem_spec = pl.BlockSpec(memory_space=pltpu.VMEM)
    smem_spec = pl.BlockSpec(memory_space=pltpu.SMEM)
    dma = pltpu.SemaphoreType.DMA
    return pl.pallas_call(
        exchange,
        out_shape=(
            jax.ShapeDtypeStruct((2, TILES, TQ, HEAD_DIM), jnp.bfloat16),
            jax.ShapeDtypeStruct((2, TOK, 2 * HEAD_DIM), jnp.bfloat16),
            jax.ShapeDtypeStruct((2, CAP, 2 * HEAD_DIM), jnp.bfloat16),
        ),
        in_specs=[smem_spec] * 2 + [any_spec] * 3 + [vmem_spec] * 2,
        out_specs=(vmem_spec, vmem_spec, any_spec),
        scratch_shapes=[
            pltpu.VMEM((32, SLICE, 4 * HEAD_DIM), jnp.bfloat16),
            pltpu.VMEM((STRIPE, 2 * GW), jnp.bfloat16),
            pltpu.VMEM((TOK, D), jnp.bfloat16),
            pltpu.VMEM((D, GW), jnp.bfloat16),
            pltpu.VMEM((2, STRIPE, GW), jnp.bfloat16),
            pltpu.VMEM((16, 2, 2, SLICE, 2 * HEAD_DIM), jnp.bfloat16),
            pltpu.VMEM((TOK, D), jnp.bfloat16),
            pltpu.VMEM((2, TOK, D), jnp.bfloat16),
            pltpu.VMEM((8, 2, SLICE, 2 * HEAD_DIM), jnp.bfloat16),
            dma((5,)),
            dma((2,)),
            dma((2,)),
            dma((16, 2)),
            dma((16, 2)),
            dma((8,)),
            dma((8,)),
            dma((4, 16)),
            dma((4, 16)),
            dma((2, 5, 4)),
            dma((2, 5, 4)),
        ],
        compiler_params=pltpu.CompilerParams(
            collective_id=0, has_side_effects=True, vmem_limit_bytes=VMEM_LIMIT
        ),
        name="exchange",
    )(lens, serve, kv, w, hidden, gain, bias)


def attend_kernel(lens, serve, q_in, own_in, kv, out, q, own, kv_buf, scores, sems, side_sems):
    d = lax.axis_index("dp")
    first = d - lax.rem(d, 2)

    def extent(s):
        length = lens[serve[first + s]]
        return length, length // STEP, (length + STEP - 1) // STEP

    def load(s, j):
        rows = pl.ds(pl.multiple_of(j * STEP, STEP), STEP)
        return pltpu.make_async_copy(kv.at[s, rows, :], kv_buf.at[s, rows, :], sems.at[s, j])

    def side_loads(s):
        return (
            pltpu.make_async_copy(q_in.at[s], q.at[s], side_sems.at[s, 0]),
            pltpu.make_async_copy(own_in.at[s], own.at[s], side_sems.at[s, 1]),
        )

    for s in range(2):
        for copy in side_loads(s):
            copy.start()

        def load_start(j, carry, s=s):
            load(s, j).start()
            return carry

        lax.fori_loop(0, extent(s)[2], load_start, 0)
    ones = jnp.ones((KB, 8), jnp.bfloat16)
    key_id = lax.broadcasted_iota(jnp.int32, (TILE, TQ), 0)
    query_id = lax.rem(lax.broadcasted_iota(jnp.int32, (TILE, TQ), 1), TILE)
    seen = (key_id // SPAN == query_id // SPAN) & (key_id <= query_id)

    def tile(i, carry):
        s = i // TILES
        t = lax.rem(i, TILES)
        length, full, blocks = extent(s)

        @pl.when(t == 0)
        def _():
            for copy in side_loads(s):
                copy.wait()

        query = q[s, t]

        def kv_rows(j):
            return pl.ds(pl.multiple_of(j * KB, KB), KB)

        def score(j, slot, masked):
            raw = lax.dot_general(
                kv_buf[s, kv_rows(j), :HEAD_DIM],
                query,
                (((1,), (1,)), ((), ())),
                preferred_element_type=jnp.float32,
            )
            if masked:
                row = j * KB + lax.broadcasted_iota(jnp.int32, (KB, 1), 0)
                raw = jnp.where(row < length, raw, -jnp.inf)
            scores[slot] = raw
            return jnp.max(raw, axis=0, keepdims=True)

        def absorb(state, raw, peak, values, ones):
            top, acc = state
            new_top = jnp.maximum(top, peak)
            weights = jnp.exp2((raw - new_top) * FOLD).astype(jnp.bfloat16)
            factor = jnp.exp2((top - new_top) * FOLD)
            wide = jnp.concatenate([values, ones], axis=1)
            acc = acc * factor + lax.dot_general(
                wide, weights, (((0,), (0,)), ((), ())), preferred_element_type=jnp.float32
            )
            return new_top, acc

        def step(j, carry, masked):
            peak, state = carry

            @pl.when((t == 0) & (j + 1 < blocks))
            def _():
                load(s, j + 1).wait()

            ahead = score(2 * j + 1, 1, masked)
            state = absorb(state, scores[0], peak, kv_buf[s, kv_rows(2 * j), HEAD_DIM:], ones)
            peak = score(jnp.minimum(2 * j + 2, 2 * blocks - 1), 0, masked)
            state = absorb(state, scores[1], ahead, kv_buf[s, kv_rows(2 * j + 1), HEAD_DIM:], ones)
            return peak, state

        @pl.when(t == 0)
        def _():
            load(s, 0).wait()

        own_rows = pl.ds(pl.multiple_of(t * TILE, TILE), TILE)
        raw = lax.dot_general(
            own[s, own_rows, :HEAD_DIM],
            query,
            (((1,), (1,)), ((), ())),
            preferred_element_type=jnp.float32,
        )
        peak = score(0, 0, False)
        raw = jnp.where(seen, raw, -jnp.inf)
        state = (
            jnp.full((1, TQ), -jnp.inf, jnp.float32),
            jnp.zeros((HEAD_DIM + 8, TQ), jnp.float32),
        )
        state = absorb(
            state, raw, jnp.max(raw, axis=0, keepdims=True), own[s, own_rows, HEAD_DIM:], ones[:TILE]
        )
        near = jnp.where(full == blocks, full, full - 1)
        work = lax.fori_loop(0, near, lambda j, c: step(j, c, False), (peak, state))
        _, state = lax.fori_loop(near, blocks, lambda j, c: step(j, c, True), work)
        _, acc = state
        result = (acc[:HEAD_DIM] * (1.0 / acc[HEAD_DIM : HEAD_DIM + 1])).astype(jnp.bfloat16)
        for h in range(GROUP):
            out[s, own_rows, h * HEAD_DIM : (h + 1) * HEAD_DIM] = result[
                :, h * TILE : (h + 1) * TILE
            ].T
        return carry

    lax.fori_loop(0, 2 * TILES, tile, 0)


def attend(lens, serve, q, own, kv):
    vmem_spec = pl.BlockSpec(memory_space=pltpu.VMEM)
    smem_spec = pl.BlockSpec(memory_space=pltpu.SMEM)
    return pl.pallas_call(
        attend_kernel,
        out_shape=jax.ShapeDtypeStruct((2, TOK, GROUP * HEAD_DIM), jnp.bfloat16),
        in_specs=[smem_spec] * 2 + [pl.BlockSpec(memory_space=pl.ANY)] * 3,
        out_specs=vmem_spec,
        scratch_shapes=[
            pltpu.VMEM((2, TILES, TQ, HEAD_DIM), jnp.bfloat16),
            pltpu.VMEM((2, TOK, 2 * HEAD_DIM), jnp.bfloat16),
            pltpu.VMEM((2, CAP, 2 * HEAD_DIM), jnp.bfloat16),
            pltpu.VMEM((2, KB, TQ), jnp.float32),
            pltpu.SemaphoreType.DMA((2, CAP // STEP)),
            pltpu.SemaphoreType.DMA((2, 2)),
        ],
        compiler_params=pltpu.CompilerParams(vmem_limit_bytes=VMEM_LIMIT),
        name="attend",
    )(lens, serve, q, own, kv)


def swap_kernel(out, result, local_sem, sems):
    y = lax.axis_index("grp")
    d = lax.axis_index("dp")
    core = lax.rem(d, 2)
    target = (y, d + 1 - 2 * core)
    width = GROUP * HEAD_DIM
    cols = pl.ds(pl.multiple_of(core * width, HEAD_DIM), width)
    keep = pltpu.make_async_copy(out.at[core], result.at[:, cols], local_sem)
    keep.start()
    barrier = pltpu.get_barrier_semaphore()
    pl.semaphore_signal(barrier, inc=1, device_id=target, device_id_type=MESH)
    pl.semaphore_wait(barrier, 1)
    copy = pltpu.make_async_remote_copy(
        src_ref=out.at[1 - core],
        dst_ref=result.at[:, cols],
        send_sem=sems.at[0],
        recv_sem=sems.at[1],
        device_id=target,
        device_id_type=MESH,
    )
    copy.start()
    copy.wait_send()
    other = pl.ds(pl.multiple_of((1 - core) * width, HEAD_DIM), width)
    pltpu.make_async_remote_copy(
        src_ref=out.at[1 - core],
        dst_ref=result.at[:, other],
        send_sem=sems.at[0],
        recv_sem=sems.at[1],
        device_id=target,
        device_id_type=MESH,
    ).wait_recv()
    keep.wait()


def swap(out):
    return pl.pallas_call(
        swap_kernel,
        out_shape=jax.ShapeDtypeStruct((TOK, 2 * GROUP * HEAD_DIM), jnp.bfloat16),
        in_specs=[pl.BlockSpec(memory_space=pl.ANY)],
        out_specs=pl.BlockSpec(memory_space=pltpu.VMEM),
        scratch_shapes=[pltpu.SemaphoreType.DMA, pltpu.SemaphoreType.DMA((2,))],
        compiler_params=pltpu.CompilerParams(
            collective_id=1, has_side_effects=True, vmem_limit_bytes=VMEM_LIMIT
        ),
        name="swap",
    )(out)


def shards(hidden, norm_gain, w_qkv, qkv_bias, kv_cache, prompt_len, serve_prompt, resp_live):
    q, own, kv = communicate(
        prompt_len, serve_prompt, kv_cache, w_qkv, hidden, norm_gain, qkv_bias
    )
    out = attend(prompt_len, serve_prompt, q, own, kv)
    keep = (jnp.arange(SPAN, dtype=jnp.int32)[None, :] < resp_live[:, None]).reshape(TOK, 1)
    return jnp.where(keep, swap(out), jnp.zeros((), jnp.bfloat16))


def solution(mesh):
    in_specs = (
        P(("grp", "dp"), None),
        P(),
        P("dp", None),
        P(),
        P(None, ("grp", "dp"), None),
        P(),
        P(),
        P(("grp", "dp")),
    )
    out_specs = P(("grp", "dp"), None)
    return jax.shard_map(shards, mesh=mesh, in_specs=in_specs, out_specs=out_specs, check_vma=False)
```

```python
import functools
import math

import jax
import jax.numpy as jnp
from jax import lax
from jax.experimental import pallas as pl
from jax.experimental.pallas import tpu as pltpu
from jax.sharding import PartitionSpec as P

D = 3584
HEADS = 14
GROUP = 7
HEAD_DIM = 128
SPAN = 16
CAP = 8192
TOK = 384
STRIPE = 112
GW = 1152
PLANE = 2048
SLICE = 64
TILE = 128
TQ = GROUP * TILE
TILES = TOK // TILE
KB = 512
STEP = 2 * KB
FIRST = 64
ROPE_BASE = 1000000.0
EPSILON = 1e-06
FOLD = math.log2(math.e) / math.sqrt(HEAD_DIM)
MESH = pl.DeviceIdType.MESH
OFFSETS = (0, 1, 3, 2)
NEAR = ((1, 0), (3, 0), (0, 1), (0, 3))
DIAGONAL = ((1, 1), (3, 3), (1, 3), (3, 1))
TIES = ((2, 1), (2, 3), (1, 2), (3, 2))
STRAIGHT = ((2, 0), (0, 2), (2, 2))
ORDER = ((0, 0),) + NEAR + DIAGONAL + STRAIGHT[:2] + TIES + STRAIGHT[2:]
VMEM_LIMIT = 64 * 1000 * 1000


def exchange(
    lens,
    serve,
    kv_in,
    w_in,
    hid_in,
    gain,
    bias,
    q_hbm,
    own_hbm,
    kv_out,
    q_out,
    own_out,
    kv,
    w,
    hid,
    w_buf,
    w_pack,
    kv_pack,
    hid_far,
    normed,
    bounce,
    local_sem,
    pair_send,
    pair_recv,
    kv_send,
    kv_recv,
    bounce_send,
    bounce_recv,
    y_send,
    y_recv,
    w_send,
    w_recv,
):
    y = lax.axis_index("grp")
    d = lax.axis_index("dp")
    core = lax.rem(d, 2)
    z = lax.rem(d // 2, 4)
    x = d // 8
    chip = d // 2
    up = lax.rem(y + 1, 4)
    down = lax.rem(y + 3, 4)
    opposite = lax.rem(y + 2, 4)
    partner = d + 1 - 2 * core

    fetch = [
        pltpu.make_async_copy(w_in, w, local_sem.at[2]),
        pltpu.make_async_copy(kv_in, kv, local_sem.at[3]),
        pltpu.make_async_copy(hid_in, hid, local_sem.at[4]),
    ]
    for copy in fetch:
        copy.start()
    barrier = pltpu.get_barrier_semaphore()

    def greet(k, carry):
        pl.semaphore_signal(
            barrier, inc=1, device_id=(y, lax.rem(d + k, 32)), device_id_type=MESH
        )
        return carry

    lax.fori_loop(1, 32, greet, 0)
    for other in (up, down):
        pl.semaphore_signal(barrier, inc=1, device_id=(other, d), device_id_type=MESH)

    width = GROUP * HEAD_DIM
    fetch[0].wait()
    for c in range(2):
        base = HEADS * HEAD_DIM + c * HEAD_DIM
        w_pack[c, :, :width] = w[:, c * width : (c + 1) * width]
        w_pack[c, :, width : width + HEAD_DIM] = w[:, base : base + HEAD_DIM]
        w_pack[c, :, width + HEAD_DIM :] = w[:, base + 2 * HEAD_DIM : base + 3 * HEAD_DIM]

    def pack(j, carry):
        for p in range(2):
            rows = kv[serve[2 * j + p]]
            for c in range(2):
                for part in range(2):
                    col = (2 * part + c) * HEAD_DIM
                    kv_pack[j, c, p, :, part * HEAD_DIM : (part + 1) * HEAD_DIM] = rows[
                        :, col : col + HEAD_DIM
                    ]
        return carry

    fetch[1].wait()
    lax.fori_loop(0, 16, pack, 0)
    fetch[2].wait()
    pl.semaphore_wait(barrier, 33)

    def stripe(row, rows):
        return w_buf.at[pl.ds(pl.multiple_of(row, 16), rows), :]

    def remote(src, dst, send, recv, target):
        return pltpu.make_async_remote_copy(
            src_ref=src,
            dst_ref=dst,
            send_sem=send,
            recv_sem=recv,
            device_id=target,
            device_id_type=MESH,
        )

    def at(px, pz, pc):
        return lax.rem(px, 4) * 8 + lax.rem(pz, 4) * 2 + pc

    def kv_rows(plane, source):
        return pl.ds(pl.multiple_of(plane * PLANE + source * SLICE, SLICE), SLICE)

    my_row = d * STRIPE
    give_w = remote(
        w_pack.at[1 - core], stripe(my_row, STRIPE), pair_send.at[0], pair_recv.at[0], (y, partner)
    )
    give_w.start()
    take_w = remote(
        w_pack.at[1 - core],
        stripe(partner * STRIPE, STRIPE),
        pair_send.at[0],
        pair_recv.at[0],
        (y, partner),
    )
    keep_w = pltpu.make_async_copy(w_pack.at[core], stripe(my_row, STRIPE), local_sem.at[0])
    keep_w.start()
    keep_kv = pltpu.make_async_copy(
        kv_pack.at[chip, core], kv_out.at[:, kv_rows(y, d), :], local_sem.at[1]
    )
    keep_kv.start()

    def order(dx, dz):
        return ORDER.index((dx, dz))

    def kv_copy(k, cs, source, target):
        return remote(
            kv_pack.at[target // 2, lax.rem(target, 2)],
            kv_out.at[:, kv_rows(y, source), :],
            kv_send.at[k, lax.rem(target, 2)],
            kv_recv.at[k, cs],
            (y, target),
        )

    def bounce_in(slot, k, far, middle):
        return remote(
            kv_pack.at[far // 2, lax.rem(far, 2)],
            bounce.at[slot],
            kv_send.at[k, lax.rem(far, 2)],
            bounce_recv.at[slot],
            (y, middle),
        )

    def bounce_out(slot, k, cs, source, target):
        return remote(
            bounce.at[slot],
            kv_out.at[:, kv_rows(y, source), :],
            bounce_send.at[slot],
            kv_recv.at[k, cs],
            (y, target),
        )

    def outgoing(dx, dz, c2):
        k = order(dx, dz)
        far = at(x + dx, z + dz, c2)
        if dx == 2 and dz % 2 == 1:
            return bounce_in(dz // 2 * 2 + core, k, far, at(x + 3, z + dz, c2))
        if dz == 2 and dx % 2 == 1:
            return bounce_in(4 + dx // 2 * 2 + core, k, far, at(x + dx, z + 3, c2))
        return kv_copy(k, core, d, far)

    def bouncing():
        for i, step in enumerate((1, 3)):
            for cs in range(2):
                slot = 2 * i + cs
                source = at(x + 1, z + 4 - step, cs)
                yield slot, bounce_out(slot, order(2, step), cs, source, at(x + 3, z, core))
                slot = 4 + 2 * i + cs
                source = at(x + 4 - step, z + 1, cs)
                yield slot, bounce_out(slot, order(step, 2), cs, source, at(x, z + 3, core))

    give_kv = kv_copy(0, core, d, partner)

    def issue(group):
        for dx, dz in group:
            for c2 in range(2):
                outgoing(dx, dz, c2).start()

    def place(h, first, second):
        if h == 0:
            return (lax.rem(first, 4) * 8 + lax.rem(second, 4) * 2) * STRIPE
        return (lax.rem(second, 4) * 8 + lax.rem(first, 4) * 2 + 1) * STRIPE

    def along(h, phase, shift):
        if (h == 0) == (phase == 1):
            return (y, at(x + shift, z, core))
        return (y, at(x, z + shift, core))

    def mine(h):
        return (x, z) if h == 0 else (z, x)

    def w_block(kind, row):
        if kind == 2:
            return stripe(row, FIRST)
        if kind == 3:
            return stripe(row + FIRST, STRIPE - FIRST)
        return stripe(row, STRIPE)

    def w_copy(h, stage, kind, row):
        phase = 1 if stage == 0 else 2
        shift = 1 if kind in (0, 2) else 3
        ref = w_block(kind, row)
        return remote(
            ref, ref, w_send.at[h, stage, kind], w_recv.at[h, stage, kind], along(h, phase, shift)
        )

    def w_row(h, stage, kind):
        first, second = mine(h)
        back = (3, 1, 2, 2)[kind]
        if stage == 0:
            return place(h, first + back, second)
        return place(h, first + OFFSETS[stage - 1], second + back)

    def w_wait(stage, kinds):
        for h in (0, 1):
            for kind in kinds:
                w_copy(h, stage, kind, w_row(h, stage, kind)).wait_recv()

    def w_start(stage):
        for h in (0, 1):
            first, second = mine(h)
            row = place(h, first, second)
            if stage > 0:
                row = place(h, first + OFFSETS[stage - 1], second)
            for kind in (0, 1):
                w_copy(h, stage, kind, row).start()

    def w_forward(stage):
        for h in (0, 1):
            for kind in (0, 1):
                w_copy(h, stage, kind + 2, w_row(h, stage, kind)).start()

    give_h = remote(hid, hid_far, pair_send.at[1], pair_recv.at[1], (y, partner))

    def chip_of(k):
        dx, dz = ORDER[k]
        return lax.rem(x + 4 - dx, 4) * 4 + lax.rem(z + 4 - dz, 4)

    def chip_rows(plane, k):
        return pl.ds(pl.multiple_of(plane * PLANE + chip_of(k) * 2 * SLICE, SLICE), 2 * SLICE)

    def y_copy(kind, k, plane):
        rows = chip_rows(plane, k)
        if kind >= 2:
            ref = kv_out.at[kind - 2, rows, :]
        else:
            ref = kv_out.at[:, rows, :]
        target = (up, d) if kind in (0, 2) else (down, d)
        return remote(ref, ref, y_send.at[kind, k], y_recv.at[kind, k], target)

    def spread(k):
        for cs in range(2):
            kv_copy(k, cs, chip_of(k) * 2 + cs, d).wait_recv()
        y_copy(0, k, y).start()
        y_copy(1, k, y).start()

    def relay(k):
        y_copy(0, k, down).wait_recv()
        y_copy(2, k, down).start()
        y_copy(1, k, up).wait_recv()
        y_copy(3, k, up).start()

    def norm(source, slot):
        scale = gain[...].astype(jnp.float32).reshape(1, D)

        def rows(i, carry):
            part = pl.ds(pl.multiple_of(i * 32, 32), 32)
            values = source[part, :].astype(jnp.float32)
            spread = lax.rsqrt(jnp.mean(values * values, axis=-1, keepdims=True) + EPSILON)
            scaled = values * spread * scale
            normed[slot, part, :] = scaled.astype(jnp.bfloat16)
            return carry

        lax.fori_loop(0, TOK // 32, rows, 0)

    def first_spread():
        keep_kv.wait()
        kv_copy(0, 1 - core, partner, d).wait_recv()
        y_copy(0, 0, y).start()
        y_copy(1, 0, y).start()

    def begin_w():
        keep_w.wait()
        take_w.wait_recv()
        w_start(0)

    def hop(stage):
        w_wait(stage, (0, 1))
        w_forward(stage)

    def bounce_all():
        for slot, copy in bouncing():
            bounce_in(slot, 0, d, d).wait_recv()
            copy.start()

    def norm_far():
        give_h.wait_recv()
        norm(hid_far, 1 - core)

    give_kv.start()
    issue(NEAR)
    issue(DIAGONAL)
    issue(TIES)
    begin_w()
    issue(STRAIGHT)
    give_h.start()
    first_spread()
    for k in range(1, 5):
        spread(k)
    bounce_all()
    for k in range(5, 9):
        spread(k)
    hop(0)
    w_start(1)
    for k in range(9, 12):
        spread(k)
    w_start(2)
    w_start(3)
    norm(hid, core)
    for k in range(12, 16):
        spread(k)
        relay(k - 12)
    for k in range(4, 6):
        relay(k)
    hop(1)
    norm_far()
    for k in range(6, 12):
        relay(k)
    w_wait(0, (2, 3))
    w_start(4)
    hop(2)
    for k in range(12, 16):
        relay(k)
    hop(3)
    hop(4)
    for stage in (1, 2, 3, 4):
        w_wait(stage, (2, 3))

    steps_range = lax.broadcasted_iota(jnp.int32, (SPAN, HEAD_DIM), 1)
    steps_range = jnp.where(
        steps_range < HEAD_DIM // 2, steps_range, steps_range - HEAD_DIM // 2
    ).astype(jnp.float32)
    inverse = jnp.exp(steps_range * (-2.0 * math.log(ROPE_BASE) / HEAD_DIM))
    flip = lax.broadcasted_iota(jnp.int32, (SPAN, HEAD_DIM), 1) < HEAD_DIM // 2
    slots = lax.broadcasted_iota(jnp.int32, (SPAN, HEAD_DIM), 0)

    bias_row = bias[...].astype(jnp.float32).reshape(1, 2 * GW)

    def bias_at(low):
        both_sides = []
        for c in range(2):
            start = c * width + low
            if low >= width:
                start = HEADS * HEAD_DIM + (low - width) * 2 + c * HEAD_DIM
            both_sides.append(bias_row[:, start : start + HEAD_DIM])
        return jnp.where(core == 0, both_sides[0], both_sides[1])

    def side(s, carry):
        length = lens[serve[d - core + s]]
        turn = (length + slots).astype(jnp.float32) * inverse
        cos = jnp.cos(turn)
        sin = jnp.sin(turn)
        sin = jnp.where(flip, -sin, sin)
        cos = jnp.broadcast_to(cos[None], (TOK // SPAN, SPAN, HEAD_DIM)).reshape(TOK, HEAD_DIM)
        sin = jnp.broadcast_to(sin[None], (TOK // SPAN, SPAN, HEAD_DIM)).reshape(TOK, HEAD_DIM)
        for low in range(0, GW, 2 * HEAD_DIM):
            high = min(low + 2 * HEAD_DIM, GW)
            part = jnp.dot(normed[s], w_buf[:, low:high], preferred_element_type=jnp.float32)
            for u in range((high - low) // HEAD_DIM):
                head = part[:, u * HEAD_DIM : (u + 1) * HEAD_DIM] + bias_at(low + u * HEAD_DIM)
                index = low // HEAD_DIM + u
                if index <= GROUP:
                    head = head * cos + pltpu.roll(head, HEAD_DIM // 2, 1) * sin
                head = head.astype(jnp.bfloat16)
                if index < GROUP:
                    for t in range(TILES):
                        q_out[s, t, index * TILE : (index + 1) * TILE, :] = head[
                            t * TILE : (t + 1) * TILE
                        ]
                else:
                    col = (index - GROUP) * HEAD_DIM
                    own_out[s, :, col : col + HEAD_DIM] = head
        return carry

    lax.fori_loop(0, 2, side, 0)
    leave = [
        pltpu.make_async_copy(q_out, q_hbm, local_sem.at[2]),
        pltpu.make_async_copy(own_out, own_hbm, local_sem.at[3]),
    ]
    for copy in leave:
        copy.start()

    for k in range(16):
        y_copy(2, k, opposite).wait_recv()
        y_copy(3, k, opposite).wait_recv()
        y_copy(0, k, y).wait_send()
        y_copy(1, k, y).wait_send()
        y_copy(2, k, down).wait_send()
        y_copy(3, k, up).wait_send()
    give_kv.wait_send()
    for dx, dz in ORDER[1:]:
        for c2 in range(2):
            outgoing(dx, dz, c2).wait_send()
    for _, copy in bouncing():
        copy.wait_send()
    for stage in range(5):
        for h in (0, 1):
            for kind in range(4):
                w_copy(h, stage, kind, w_row(h, stage, kind)).wait_send()
    for copy in leave:
        copy.wait()
    give_w.wait_send()
    give_h.wait_send()


def communicate(lens, serve, kv, w, hidden, gain, bias):
    any_spec = pl.BlockSpec(memory_space=pl.ANY)
    vmem_spec = pl.BlockSpec(memory_space=pltpu.VMEM)
    smem_spec = pl.BlockSpec(memory_space=pltpu.SMEM)
    dma = pltpu.SemaphoreType.DMA
    return pl.pallas_call(
        exchange,
        out_shape=(
            jax.ShapeDtypeStruct((2, TILES, TQ, HEAD_DIM), jnp.bfloat16),
            jax.ShapeDtypeStruct((2, TOK, 2 * HEAD_DIM), jnp.bfloat16),
            jax.ShapeDtypeStruct((2, CAP, 2 * HEAD_DIM), jnp.bfloat16),
        ),
        in_specs=[smem_spec] * 2 + [any_spec] * 3 + [vmem_spec] * 2,
        out_specs=(any_spec, any_spec, any_spec),
        scratch_shapes=[
            pltpu.VMEM((2, TILES, TQ, HEAD_DIM), jnp.bfloat16),
            pltpu.VMEM((2, TOK, 2 * HEAD_DIM), jnp.bfloat16),
            pltpu.VMEM((32, SLICE, 4 * HEAD_DIM), jnp.bfloat16),
            pltpu.VMEM((STRIPE, 2 * GW), jnp.bfloat16),
            pltpu.VMEM((TOK, D), jnp.bfloat16),
            pltpu.VMEM((D, GW), jnp.bfloat16),
            pltpu.VMEM((2, STRIPE, GW), jnp.bfloat16),
            pltpu.VMEM((16, 2, 2, SLICE, 2 * HEAD_DIM), jnp.bfloat16),
            pltpu.VMEM((TOK, D), jnp.bfloat16),
            pltpu.VMEM((2, TOK, D), jnp.bfloat16),
            pltpu.VMEM((8, 2, SLICE, 2 * HEAD_DIM), jnp.bfloat16),
            dma((5,)),
            dma((2,)),
            dma((2,)),
            dma((16, 2)),
            dma((16, 2)),
            dma((8,)),
            dma((8,)),
            dma((4, 16)),
            dma((4, 16)),
            dma((2, 5, 4)),
            dma((2, 5, 4)),
        ],
        compiler_params=pltpu.CompilerParams(
            collective_id=0, has_side_effects=True, vmem_limit_bytes=VMEM_LIMIT
        ),
        name="exchange",
    )(lens, serve, kv, w, hidden, gain, bias)


def attend_kernel(
    lens, serve, q_in, own_in, kv, out_hbm, out, q, own, kv_buf, scores, sems, side_sems, out_sems
):
    d = lax.axis_index("dp")
    first = d - lax.rem(d, 2)

    def extent(s):
        length = lens[serve[first + s]]
        return length, length // STEP, (length + STEP - 1) // STEP

    def load(s, j):
        rows = pl.ds(pl.multiple_of(j * STEP, STEP), STEP)
        return pltpu.make_async_copy(kv.at[s, rows, :], kv_buf.at[s, rows, :], sems.at[s, j])

    def side_loads(s):
        return (
            pltpu.make_async_copy(q_in.at[s], q.at[s], side_sems.at[s, 0]),
            pltpu.make_async_copy(own_in.at[s], own.at[s], side_sems.at[s, 1]),
        )

    def leave(s):
        return pltpu.make_async_copy(out.at[s], out_hbm.at[s], out_sems.at[s])

    for s in range(2):
        for copy in side_loads(s):
            copy.start()

        def load_start(j, carry, s=s):
            load(s, j).start()
            return carry

        lax.fori_loop(0, extent(s)[2], load_start, 0)
    ones = jnp.ones((KB, 8), jnp.bfloat16)
    key_id = lax.broadcasted_iota(jnp.int32, (TILE, TQ), 0)
    query_id = lax.rem(lax.broadcasted_iota(jnp.int32, (TILE, TQ), 1), TILE)
    seen = (key_id // SPAN == query_id // SPAN) & (key_id <= query_id)

    def tile(i, carry):
        s = i // TILES
        t = lax.rem(i, TILES)
        length, full, blocks = extent(s)

        @pl.when(t == 0)
        def _():
            for copy in side_loads(s):
                copy.wait()

        query = q[s, t]

        def kv_rows(j):
            return pl.ds(pl.multiple_of(j * KB, KB), KB)

        def score(j, slot, masked):
            raw = lax.dot_general(
                kv_buf[s, kv_rows(j), :HEAD_DIM],
                query,
                (((1,), (1,)), ((), ())),
                preferred_element_type=jnp.float32,
            )
            if masked:
                row = j * KB + lax.broadcasted_iota(jnp.int32, (KB, 1), 0)
                raw = jnp.where(row < length, raw, -jnp.inf)
            scores[slot] = raw
            return jnp.max(raw, axis=0, keepdims=True)

        def absorb(state, raw, peak, values, ones):
            top, acc = state
            new_top = jnp.maximum(top, peak)
            weights = jnp.exp2((raw - new_top) * FOLD).astype(jnp.bfloat16)
            factor = jnp.exp2((top - new_top) * FOLD)
            wide = jnp.concatenate([values, ones], axis=1)
            acc = acc * factor + lax.dot_general(
                wide, weights, (((0,), (0,)), ((), ())), preferred_element_type=jnp.float32
            )
            return new_top, acc

        def step(j, carry, masked):
            peak, state = carry

            @pl.when((t == 0) & (j + 1 < blocks))
            def _():
                load(s, j + 1).wait()

            ahead = score(2 * j + 1, 1, masked)
            state = absorb(state, scores[0], peak, kv_buf[s, kv_rows(2 * j), HEAD_DIM:], ones)
            peak = score(jnp.minimum(2 * j + 2, 2 * blocks - 1), 0, masked)
            state = absorb(state, scores[1], ahead, kv_buf[s, kv_rows(2 * j + 1), HEAD_DIM:], ones)
            return peak, state

        @pl.when(t == 0)
        def _():
            load(s, 0).wait()

        own_rows = pl.ds(pl.multiple_of(t * TILE, TILE), TILE)
        raw = lax.dot_general(
            own[s, own_rows, :HEAD_DIM],
            query,
            (((1,), (1,)), ((), ())),
            preferred_element_type=jnp.float32,
        )
        peak = score(0, 0, False)
        raw = jnp.where(seen, raw, -jnp.inf)
        state = (
            jnp.full((1, TQ), -jnp.inf, jnp.float32),
            jnp.zeros((HEAD_DIM + 8, TQ), jnp.float32),
        )
        state = absorb(
            state, raw, jnp.max(raw, axis=0, keepdims=True), own[s, own_rows, HEAD_DIM:], ones[:TILE]
        )
        near = jnp.where(full == blocks, full, full - 1)
        work = lax.fori_loop(0, near, lambda j, c: step(j, c, False), (peak, state))
        _, state = lax.fori_loop(near, blocks, lambda j, c: step(j, c, True), work)
        _, acc = state
        result = (acc[:HEAD_DIM] * (1.0 / acc[HEAD_DIM : HEAD_DIM + 1])).astype(jnp.bfloat16)
        for h in range(GROUP):
            out[s, own_rows, h * HEAD_DIM : (h + 1) * HEAD_DIM] = result[
                :, h * TILE : (h + 1) * TILE
            ].T

        @pl.when(t == TILES - 1)
        def _():
            leave(s).start()

        return carry

    lax.fori_loop(0, 2 * TILES, tile, 0)
    for s in range(2):
        leave(s).wait()


def attend(lens, serve, q, own, kv):
    smem_spec = pl.BlockSpec(memory_space=pltpu.SMEM)
    return pl.pallas_call(
        attend_kernel,
        out_shape=jax.ShapeDtypeStruct((2, TOK, GROUP * HEAD_DIM), jnp.bfloat16),
        in_specs=[smem_spec] * 2 + [pl.BlockSpec(memory_space=pl.ANY)] * 3,
        out_specs=pl.BlockSpec(memory_space=pl.ANY),
        scratch_shapes=[
            pltpu.VMEM((2, TOK, GROUP * HEAD_DIM), jnp.bfloat16),
            pltpu.VMEM((2, TILES, TQ, HEAD_DIM), jnp.bfloat16),
            pltpu.VMEM((2, TOK, 2 * HEAD_DIM), jnp.bfloat16),
            pltpu.VMEM((2, CAP, 2 * HEAD_DIM), jnp.bfloat16),
            pltpu.VMEM((2, KB, TQ), jnp.float32),
            pltpu.SemaphoreType.DMA((2, CAP // STEP)),
            pltpu.SemaphoreType.DMA((2, 2)),
            pltpu.SemaphoreType.DMA((2,)),
        ],
        compiler_params=pltpu.CompilerParams(vmem_limit_bytes=VMEM_LIMIT),
        name="attend",
    )(lens, serve, q, own, kv)


def swap_kernel(out, result, local_sem, sems):
    y = lax.axis_index("grp")
    d = lax.axis_index("dp")
    core = lax.rem(d, 2)
    target = (y, d + 1 - 2 * core)
    width = GROUP * HEAD_DIM
    cols = pl.ds(pl.multiple_of(core * width, HEAD_DIM), width)
    keep = pltpu.make_async_copy(out.at[core], result.at[:, cols], local_sem)
    keep.start()
    barrier = pltpu.get_barrier_semaphore()
    pl.semaphore_signal(barrier, inc=1, device_id=target, device_id_type=MESH)
    pl.semaphore_wait(barrier, 1)
    copy = pltpu.make_async_remote_copy(
        src_ref=out.at[1 - core],
        dst_ref=result.at[:, cols],
        send_sem=sems.at[0],
        recv_sem=sems.at[1],
        device_id=target,
        device_id_type=MESH,
    )
    copy.start()
    copy.wait_send()
    other = pl.ds(pl.multiple_of((1 - core) * width, HEAD_DIM), width)
    pltpu.make_async_remote_copy(
        src_ref=out.at[1 - core],
        dst_ref=result.at[:, other],
        send_sem=sems.at[0],
        recv_sem=sems.at[1],
        device_id=target,
        device_id_type=MESH,
    ).wait_recv()
    keep.wait()


def swap(out):
    return pl.pallas_call(
        swap_kernel,
        out_shape=jax.ShapeDtypeStruct((TOK, 2 * GROUP * HEAD_DIM), jnp.bfloat16),
        in_specs=[pl.BlockSpec(memory_space=pl.ANY)],
        out_specs=pl.BlockSpec(memory_space=pltpu.VMEM),
        scratch_shapes=[pltpu.SemaphoreType.DMA, pltpu.SemaphoreType.DMA((2,))],
        compiler_params=pltpu.CompilerParams(
            collective_id=1, has_side_effects=True, vmem_limit_bytes=VMEM_LIMIT
        ),
        name="swap",
    )(out)


def shards(hidden, norm_gain, w_qkv, qkv_bias, kv_cache, prompt_len, serve_prompt, resp_live):
    q, own, kv = communicate(
        prompt_len, serve_prompt, kv_cache, w_qkv, hidden, norm_gain, qkv_bias
    )
    out = attend(prompt_len, serve_prompt, q, own, kv)
    keep = (jnp.arange(SPAN, dtype=jnp.int32)[None, :] < resp_live[:, None]).reshape(TOK, 1)
    return jnp.where(keep, swap(out), jnp.zeros((), jnp.bfloat16))


def solution(mesh):
    in_specs = (
        P(("grp", "dp"), None),
        P(),
        P("dp", None),
        P(),
        P(None, ("grp", "dp"), None),
        P(),
        P(),
        P(("grp", "dp")),
    )
    out_specs = P(("grp", "dp"), None)
    return jax.shard_map(shards, mesh=mesh, in_specs=in_specs, out_specs=out_specs, check_vma=False)
```
